256 devices in a mesh: section: 4 (over x), expert: 64 (over y, z, core).
Axes of the slice: x: 4, y: 4, z: 8, core: 2. Of those that a mesh axis runs over, the one named last changes fastest.
Arguments:
- tokens: bfloat16 [2, 4096, 2560], P(None, 'expert'), may hold values from -6 to 6
- norm_gain: float32 [4, 2560], P('section'), may hold values from 0.1 to 1.9
- w_gate: bfloat16 [4, 2560, 24576], P('section', None, 'expert'), may hold values from -0.125 to 0.125
- w_up: bfloat16 [4, 2560, 24576], P('section', None, 'expert'), may hold values from -0.125 to 0.125
- w_down: bfloat16 [4, 24576, 2560], P('section', 'expert'), may hold values from -0.21875 to 0.21875
- route_ids: int32 [4, 2, 4096, 2], P('section', None, 'expert'), may hold values from 0 to 31, all different within a row; in each aligned block of 64 rows (0 to 63, 64 to 127, ..., all dimensions but the last counted through in order) at most 6 rows name the same one
- route_gates: float32 [4, 2, 4096, 2], P('section', None, 'expert'), may hold values from 0.1 to 0.6
Outputs:
- input_grads: bfloat16 [4, 2, 4096, 2560], P('section', None, 'expert')
The draws below stay inside these ranges and needn't reach their ends.
Inputs may be any that keep to these rules, and one draw needn't show every extreme that they name: `route_ids`: each row names 2 different experts. In each aligned block of 64 rows (one device's tokens of one microbatch in one layer) no expert is named by more than 6 rows, and in some block an expert is named by exactly 6 rows.
All inputs are finite; a program needn't handle non-finite values.
Results may differ from the reference program's by a relative error of at most 0.02.
Values may be sent and summed in bfloat16 or wider, within the bound.
A program may use at most 128 MiB of HBM per device.

```python
import math
import jax
import jax.numpy as jnp
import numpy as np
from jax import lax

D = 2560
H = 768
TOP = 2
MICRO = 2
TOK_DEV = 64
EXPERTS = 32
CAP = 6
TOKENS = 4096
N_SECTION = 4
N_EXPERT = 64


def block_levels(key, dims, pieces, smallest, largest):
    def one(axis_at, shards_of):
        draws = jax.random.uniform(jax.random.fold_in(jax.random.fold_in(key, 6), axis_at), (shards_of,), jnp.float32, smallest / len(pieces), largest / len(pieces))
        return jnp.repeat(jnp.exp(draws), dims[axis_at] // shards_of).reshape((-1,) + (1,) * (len(dims) - axis_at - 1))

    factor_of = one(*pieces[0])
    for cut in pieces[1:]:
        factor_of = factor_of * one(*cut)
    return factor_of


def routed_block(key, own, number, rows, number_of, top, bound, lean):
    ranking = jax.random.permutation(key, number_of)
    packed, usual = portions_of(number_of, rows * top, bound, lean, True), portions_of(number_of, rows * top, bound, lean, False)
    places = jnp.arange(number_of)

    def named(lengths, turn):
        used = int((lengths > 0).sum())
        fixed = max(1, used // 4)
        shifted = fixed + (places - fixed + turn * (used - fixed)) % max(1, number_of - fixed)
        return jnp.zeros((number_of,), jnp.int32).at[ranking[jnp.where(places < fixed, places, shifted)]].set(jnp.asarray(lengths, jnp.int32))

    lengths = jnp.where(number % 4 == 0, named(packed, number // 4), named(usual, number - number // 4 - 1))
    mixed = jax.random.permutation(jax.random.fold_in(own, 3), number_of)
    source_of, receiver = mixed[0:number_of // 2 * 2:2], mixed[1:number_of // 2 * 2:2]
    margin = jnp.minimum(lengths[source_of] - 1, bound - lengths[receiver]) // 2
    margin = jnp.where((source_of == ranking[0]) | (receiver == ranking[0]) | (lengths[receiver] == 0), 0, jnp.maximum(margin, 0))
    shifted = jax.random.randint(jax.random.fold_in(own, 4), (number_of // 2,), 0, 1 << 20) % (margin + 1)
    lengths = lengths.at[source_of].add(-shifted).at[receiver].add(shifted)
    members = jnp.searchsorted(jnp.cumsum(lengths), jnp.arange(rows * top), side="right").astype(jnp.int32)
    grid = members.reshape(top, rows).T
    grid = grid[jax.random.permutation(jax.random.fold_in(own, 1), rows)]
    turn = jax.random.randint(jax.random.fold_in(own, 2), (rows, 1), 0, top)
    return jnp.take_along_axis(grid, (jnp.arange(top)[None, :] + turn) % top, axis=1)


def portions_of(count, total, limit, slope, full):
    weights = [(1 << 20) // math.isqrt(grade ** slope) + 1 for grade in range(1, count + 1)]
    largest = limit if full else min(limit, max(-(-total // count), total * weights[0] // sum(weights)))
    least = 1 if total - largest >= count - 1 else 0
    given, surplus = [largest] + [least] * (count - 1), total - largest - least * (count - 1)
    while surplus > 0:
        free = [i for i in range(1, count) if given[i] < largest] or [i for i in range(1, count) if given[i] < limit]
        whole, remaining = sum([weights[i] for i in free]), surplus
        for i in free:
            extra = min(limit - given[i], max(1, remaining * weights[i] // whole), surplus)
            given[i] = given[i] + extra
            surplus = surplus - extra
    return np.array(given)


def centred(rng, shape, scale, bound, cuts=(), kind=jnp.bfloat16):
    drawn = jax.random.normal(rng, shape, jnp.float32) * scale
    if len(cuts) > 0:
        drawn = block_levels(rng, shape, cuts, -0.22, 0.18) * drawn
    return jnp.clip(drawn, min=-bound, max=bound).astype(kind)


def setup_inputs(seed: int = 0) -> dict:
    splits = jax.random.split(jax.random.key(seed), 8)
    tokens = centred(splits[0], (MICRO, TOKENS, D), 1.0, 6.0, ((1, 64),))
    norm_gain = jnp.clip(1.0 + 0.18 * jax.random.normal(splits[1], (N_SECTION, D), jnp.float32), 0.1, 1.9)
    w_gate = centred(splits[2], (N_SECTION, D, EXPERTS * H), D ** -0.5, 0.125, ((0, 4), (2, 64)))
    w_up = centred(splits[3], (N_SECTION, D, EXPERTS * H), D ** -0.5, 0.125, ((0, 4), (2, 64)))
    w_down = centred(splits[4], (N_SECTION, EXPERTS * H, D), H ** -0.5, 0.21875, ((0, 4), (1, 64)))
    route_ids_keys = jax.random.split(jax.random.fold_in(splits[5], 1), N_SECTION * MICRO * TOKENS // TOK_DEV)
    route_ids_turns = jax.random.permutation(jax.random.fold_in(splits[5], 3), N_SECTION * MICRO * TOKENS // TOK_DEV)
    route_ids = jax.vmap(lambda own, number: routed_block(jax.random.fold_in(splits[5], 2), own, number, TOK_DEV, EXPERTS, TOP, CAP, 2))(route_ids_keys, route_ids_turns).reshape((N_SECTION, MICRO, TOKENS, TOP))
    route_gates = jnp.clip(jnp.exp(math.log(0.6) - 1.7917595 * jax.random.uniform(splits[6], (N_SECTION, MICRO, TOKENS, TOP), jnp.float32) ** block_levels(splits[6], (N_SECTION, MICRO, TOKENS, TOP), ((0, 4), (2, 64)), -0.2, 0.2)), 0.1, 0.6)
    return dict(tokens=tokens, norm_gain=norm_gain, w_gate=w_gate, w_up=w_up, w_down=w_down, route_ids=route_ids, route_gates=route_gates)


EPS = 1e-06

def normalize(h_rows, gain_vec):
    widened = h_rows.astype(jnp.float32)
    inv_rms = lax.rsqrt(lax.optimization_barrier(jnp.mean(widened * widened, axis=-1, keepdims=True)) + EPS)
    return (widened * inv_rms * gain_vec).astype(jnp.bfloat16)

def norm_grad(h_rows, gain_vec, upstream):
    widened = h_rows.astype(jnp.float32)
    inv_rms = lax.rsqrt(lax.optimization_barrier(jnp.mean(widened * widened, axis=-1, keepdims=True)) + EPS)
    weighted = gain_vec * upstream
    projected = lax.optimization_barrier(jnp.mean(widened * weighted, axis=-1, keepdims=True))
    return inv_rms * weighted - widened * inv_rms * inv_rms * inv_rms * projected

def targets_of(route_rows):
    blocks = MICRO * N_EXPERT
    flattened = route_rows.reshape(blocks, TOK_DEV * TOP)
    onehot = (flattened[:, :, None] == jnp.arange(EXPERTS, dtype=jnp.int32)[None, None, :]).astype(jnp.int32)
    before = jnp.cumsum(onehot, axis=1) - onehot
    position = lax.optimization_barrier(jnp.sum(before * onehot, axis=-1))
    offset = jnp.arange(blocks, dtype=jnp.int32)[:, None] * CAP
    return (flattened * (blocks * CAP) + offset + position).reshape(-1).astype(jnp.int32)

def dispatch(pair_rows, targets):
    slots_all = EXPERTS * MICRO * N_EXPERT * CAP
    filled = jnp.zeros((slots_all, D), jnp.bfloat16).at[targets].set(pair_rows)
    return filled.reshape(EXPERTS, MICRO * N_EXPERT * CAP, D)

def expert_forward(operands):
    arrived, gate_mat, up_mat, down_mat = operands
    half_width = H // 2
    pre_gate = jnp.dot(arrived, gate_mat, preferred_element_type=jnp.float32)
    pre_up = jnp.dot(arrived, up_mat, preferred_element_type=jnp.float32)
    hidden = (pre_gate * jax.nn.sigmoid(pre_gate) * pre_up).astype(jnp.bfloat16)
    first = jnp.dot(hidden[:, :half_width], down_mat[:half_width], preferred_element_type=jnp.float32).astype(jnp.bfloat16)
    second = jnp.dot(hidden[:, half_width:], down_mat[half_width:], preferred_element_type=jnp.float32).astype(jnp.bfloat16)
    return (jnp.stack([first, second]), pre_gate, pre_up)

def expert_backward(operands):
    arrived, pre_gate, pre_up, gate_mat, up_mat, down_mat = operands
    half_width = H // 2
    grad_hidden = jnp.dot(arrived, down_mat.T, preferred_element_type=jnp.float32)
    logistic = jax.nn.sigmoid(pre_gate)
    grad_gate = (grad_hidden * pre_up * logistic * (1.0 + pre_gate * (1.0 - logistic))).astype(jnp.bfloat16)
    grad_up = (grad_hidden * pre_gate * logistic).astype(jnp.bfloat16)
    first = jnp.dot(grad_gate[:, :half_width], gate_mat[:, :half_width].T, preferred_element_type=jnp.float32) + jnp.dot(grad_up[:, :half_width], up_mat[:, :half_width].T, preferred_element_type=jnp.float32)
    second = jnp.dot(grad_gate[:, half_width:], gate_mat[:, half_width:].T, preferred_element_type=jnp.float32) + jnp.dot(grad_up[:, half_width:], up_mat[:, half_width:].T, preferred_element_type=jnp.float32)
    return jnp.stack([first.astype(jnp.bfloat16), second.astype(jnp.bfloat16)])

def combine_halves(result, targets):
    halves = result.transpose(1, 0, 2, 3).reshape(2, -1, D)
    picked = halves[:, targets].astype(jnp.float32)
    return picked[0] + picked[1]

def reference(tokens, norm_gain, w_gate, w_up, w_down, route_ids, route_gates):
    rows_all = MICRO * TOKENS
    h_rows = tokens.reshape(rows_all, D)
    inputs = []
    gate_list = []
    up_list = []
    target_list = []
    for layer_index in range(N_SECTION):
        gate_all = w_gate[layer_index].reshape(D, EXPERTS, H).transpose(1, 0, 2)
        up_all = w_up[layer_index].reshape(D, EXPERTS, H).transpose(1, 0, 2)
        down_all = w_down[layer_index].reshape(EXPERTS, H, D)
        targets = targets_of(route_ids[layer_index].reshape(rows_all, TOP))
        normed = normalize(h_rows, norm_gain[layer_index])
        filled = dispatch(jnp.repeat(normed, TOP, axis=0), targets)
        result, pre_gate, pre_up = lax.map(expert_forward, (filled, gate_all, up_all, down_all))
        picked = combine_halves(result, targets).reshape(rows_all, TOP, D)
        gates_now = route_gates[layer_index].reshape(rows_all, TOP)
        mixture = lax.optimization_barrier(jnp.sum(gates_now[:, :, None] * picked, axis=1))
        inputs.append(h_rows)
        gate_list.append(pre_gate)
        up_list.append(pre_up)
        target_list.append(targets)
        h_rows = (h_rows.astype(jnp.float32) + mixture).astype(jnp.bfloat16)
    upstream = h_rows
    grad_list = []
    for layer_index in range(N_SECTION - 1, -1, -1):
        gate_all = w_gate[layer_index].reshape(D, EXPERTS, H).transpose(1, 0, 2)
        up_all = w_up[layer_index].reshape(D, EXPERTS, H).transpose(1, 0, 2)
        down_all = w_down[layer_index].reshape(EXPERTS, H, D)
        gates_now = route_gates[layer_index].reshape(rows_all, TOP)
        scaled = (gates_now[:, :, None] * upstream[:, None, :].astype(jnp.float32)).astype(jnp.bfloat16)
        filled = dispatch(scaled.reshape(-1, D), target_list[layer_index])
        returned = lax.map(expert_backward, (filled, gate_list[layer_index], up_list[layer_index], gate_all, up_all, down_all))
        picked = combine_halves(returned, target_list[layer_index]).reshape(rows_all, TOP, D)
        summed = lax.optimization_barrier(jnp.sum(picked, axis=1))
        upstream = (upstream.astype(jnp.float32) + norm_grad(inputs[layer_index], norm_gain[layer_index], summed)).astype(jnp.bfloat16)
        grad_list.append(upstream)
    ordered = grad_list[::-1]
    return jnp.stack(ordered).reshape(N_SECTION, MICRO, TOKENS, D)
```

```python
import functools

import jax
import jax.numpy as jnp
from jax import lax
from jax.experimental import pallas as pl
from jax.experimental.pallas import tpu as pltpu
from jax.sharding import PartitionSpec as P

EPS = 1e-06
PARTS = 4
MESH = pl.DeviceIdType.MESH
F32 = jnp.float32
BF16 = jnp.bfloat16


def mm(a, b):
    return jnp.dot(a, b, preferred_element_type=F32)


def mm_nt(a, b):
    return lax.dot_general(a, b, (((1,), (1,)), ((), ())), preferred_element_type=F32)


def kernel(
    dims,
    tokens_ref,
    gain_ref,
    route_row_ref,
    route_col_ref,
    gate_col_ref,
    perm_ref,
    perm_t_ref,
    w_gate_ref,
    w_up_ref,
    w_down_ref,
    out_ref,
    wg,
    wu,
    wd,
    h_in,
    h_out,
    g_in,
    g_out,
    send_a,
    recv_a,
    send_b,
    recv_b,
    spread,
    collect,
    stage,
    pieces,
    rows,
    pre_g,
    pre_u,
    act_a,
    act_b,
    w_local,
    w_send,
    w_recv,
    a_send,
    a_recv,
    b_send,
    b_recv,
    x_send,
    x_recv,
):
    sections, chips, cap, tok, width, micro, groups, half = dims
    blk = PARTS * cap
    part = width // PARTS
    per = chips // groups
    grp_rows = per * cap
    all_rows = chips * cap
    hidden = 2 * half
    step = 256
    s = lax.axis_index("section")
    ex = lax.axis_index("expert")
    core = lax.rem(ex, 2)
    chip = lax.div(ex, 2)
    mate = 2 * chip + (1 - core)
    my_group = lax.div(chip, per)

    def other(j):
        return lax.rem(chip + j, chips)

    barrier = pltpu.get_barrier_semaphore()

    def greet(j, carry):
        pl.semaphore_signal(
            barrier, inc=1, device_id={"expert": 2 * other(j) + core}, device_id_type=MESH
        )
        return carry

    lax.fori_loop(1, chips, greet, 0)
    pl.semaphore_signal(barrier, inc=1, device_id={"expert": mate}, device_id_type=MESH)

    @pl.when(s > 0)
    def _():
        pl.semaphore_signal(barrier, inc=1, device_id={"section": s - 1}, device_id_type=MESH)

    @pl.when(s < sections - 1)
    def _():
        pl.semaphore_signal(barrier, inc=1, device_id={"section": s + 1}, device_id_type=MESH)

    local = [
        pltpu.make_async_copy(w_gate_ref, wg.at[:, :half], w_local.at[0]),
        pltpu.make_async_copy(w_up_ref, wu.at[:, :half], w_local.at[1]),
        pltpu.make_async_copy(w_down_ref, wd.at[:half, :], w_local.at[2]),
    ]
    for copy in local:
        copy.start()

    ahead = lax.convert_element_type(s > 0, jnp.int32)
    behind = lax.convert_element_type(s < sections - 1, jnp.int32)
    pl.semaphore_wait(barrier, chips + ahead + behind)

    remote = [
        pltpu.make_async_remote_copy(
            src, dst, w_send.at[i], w_recv.at[i], device_id={"expert": mate}, device_id_type=MESH
        )
        for i, (src, dst) in enumerate(
            (
                (w_gate_ref, wg.at[:, half:]),
                (w_up_ref, wu.at[:, half:]),
                (w_down_ref, wd.at[half:, :]),
            )
        )
    ]
    for copy in remote:
        copy.start()

    for m in range(micro):
        for k in range(2):
            at = k * PARTS * tok
            n = PARTS * tok
            lane = route_row_ref[m, :, at : at + n]
            ids = lax.broadcasted_iota(jnp.int32, (chips * blk, n), 0)
            spread[m, :, at : at + n] = jnp.where(ids == lane, 1.0, 0.0).astype(BF16)
            sub = route_col_ref[m, at : at + n, :]
            ids = lax.broadcasted_iota(jnp.int32, (n, chips * blk), 1)
            collect[m, at : at + n, :] = jnp.where(ids == sub, 1.0, 0.0).astype(BF16)

    def send_block(u, d, src, dst, send_sem, recv_sem):
        return pltpu.make_async_remote_copy(
            src.at[u, d],
            dst.at[u, chip],
            send_sem.at[u],
            recv_sem.at[u, my_group],
            device_id={"expert": 2 * d + core},
            device_id_type=MESH,
        )

    def scatter(u, src, dst, send_sem, recv_sem):
        def one(j, carry):
            send_block(u, other(j), src, dst, send_sem, recv_sem).start()
            return carry

        lax.fori_loop(1, chips, one, 0)
        pltpu.make_async_copy(src.at[u, chip], dst.at[u, chip], recv_sem.at[u, my_group]).start()

    def group_wait(u, g, dst, recv_sem):
        view = dst.at[u, pl.ds(g * per, per)]
        pltpu.make_async_copy(view, view, recv_sem.at[u, g]).wait()

    def arrive(u):
        def one(i, carry):
            g = lax.rem(my_group + i, groups)
            group_wait(u, g, recv_a, a_recv)
            got = recv_a[u, pl.ds(g * per, per)].astype(F32).reshape(per * blk, part).astype(BF16)
            sorted_rows = mm(perm_ref[...], got).astype(BF16)
            for q in range(PARTS):
                rows[pl.ds(g * grp_rows, grp_rows), q * part : (q + 1) * part] = sorted_rows[
                    q * grp_rows : (q + 1) * grp_rows
                ]
            return carry

        lax.fori_loop(0, groups, one, 0)

    def give_back(u):
        def one(g, carry):
            got = mm(perm_t_ref[...], pieces[g])
            send_b[u, pl.ds(g * per, per)] = got.reshape(per, blk, part).astype(BF16)
            return carry

        lax.fori_loop(0, groups, one, 0)
        scatter(u, send_b, recv_b, b_send, b_recv)

    def wait_back(u):
        def one(g, carry):
            group_wait(u, g, recv_b, b_recv)
            return carry

        lax.fori_loop(0, groups, one, 0)
        return recv_b[u].astype(F32).reshape(chips * blk, part).astype(BF16)

    def put_pieces(q, value):
        for g in range(groups):
            pieces[g, pl.ds(q * grp_rows, grp_rows), :] = value[g * grp_rows : (g + 1) * grp_rows]

    def inverse_rms(h):
        total = jnp.sum(jnp.sum(h * h, axis=-1, keepdims=True), axis=0)
        return lax.rsqrt(total / width + EPS)

    def hop(buf_src, buf_dst, m, index, to):
        return pltpu.make_async_remote_copy(
            buf_src.at[m],
            buf_dst.at[m],
            x_send.at[index],
            x_recv.at[index],
            device_id={"section": to},
            device_id_type=MESH,
        )

    def forward(m, carry):
        u = m

        @pl.when(s == 0)
        def _():
            for q in range(PARTS):
                h_in[m, q] = tokens_ref[m, :, q * part : (q + 1) * part]

        @pl.when(s > 0)
        def _():
            hop(h_out, h_in, m, m, s).wait_recv()

        h = h_in[m].astype(F32)
        inv = inverse_rms(h)
        for q in range(PARTS):
            stage[pl.ds(q * tok, tok), :] = (
                h_in[m, q].astype(F32) * inv * gain_ref[:, q * part : (q + 1) * part]
            ).astype(BF16)
        n = PARTS * tok
        sel = spread[m, :, :n] + spread[m, :, n:]
        out = mm(sel, stage[:n, :])
        send_a[u] = out.reshape(chips, blk, part).astype(BF16)
        scatter(u, send_a, recv_a, a_send, a_recv)

        @pl.when(m == 0)
        def _():
            for copy in local:
                copy.wait()
            for copy in remote:
                copy.wait_recv()

        arrive(u)

        def first(i, carry):
            at = pl.ds(pl.multiple_of(i * step, step), step)
            gate = mm(rows[...], wg[:, at])
            up = mm(rows[...], wu[:, at])
            pre_g[m, i] = gate
            pre_u[m, i] = up
            act_a[:, at] = (gate * jax.nn.sigmoid(gate) * up).astype(BF16)
            return carry

        lax.fori_loop(0, hidden // step, first, 0)

        def second(q, carry):
            at = pl.ds(pl.multiple_of(q * part, part), part)
            put_pieces(q, mm(act_a[...], wd[:, at]).astype(BF16))
            return carry

        lax.fori_loop(0, PARTS, second, 0)
        give_back(u)
        back = wait_back(u)
        picked = mm(collect[m], back) * gate_col_ref[m]
        mixture = picked[:n] + picked[n:]
        h_out[m] = (h_in[m].astype(F32) + mixture.reshape(PARTS, tok, part)).astype(BF16)

        @pl.when(s < sections - 1)
        def _():
            hop(h_out, h_in, m, m, s + 1).start()

        return carry

    lax.fori_loop(0, micro, forward, 0)

    def backward(m, carry):
        u = micro + m

        @pl.when(s == sections - 1)
        def _():
            g_in[m] = h_out[m]

        @pl.when(s < sections - 1)
        def _():
            hop(g_out, g_in, m, micro + m, s).wait_recv()

        n = PARTS * tok
        upstream = g_in[m].astype(F32).reshape(n, part)
        stage[:n, :] = (gate_col_ref[m, :n] * upstream).astype(BF16)
        stage[n:, :] = (gate_col_ref[m, n:] * upstream).astype(BF16)
        out = mm(spread[m], stage[...])
        send_a[u] = out.reshape(chips, blk, part).astype(BF16)
        scatter(u, send_a, recv_a, a_send, a_recv)
        arrive(u)

        def first(i, carry):
            at = pl.ds(pl.multiple_of(i * step, step), step)
            grad = mm_nt(rows[...], wd[at, :])
            gate = pre_g[m, i]
            up = pre_u[m, i]
            logistic = jax.nn.sigmoid(gate)
            act_a[:, at] = (grad * up * logistic * (1.0 + gate * (1.0 - logistic))).astype(BF16)
            act_b[:, at] = (grad * gate * logistic).astype(BF16)
            return carry

        lax.fori_loop(0, hidden // step, first, 0)

        def second(q, carry):
            at = pl.ds(pl.multiple_of(q * part, part), part)
            value = mm_nt(act_a[...], wg[at, :]) + mm_nt(act_b[...], wu[at, :])
            put_pieces(q, value.astype(BF16))
            return carry

        lax.fori_loop(0, PARTS, second, 0)
        give_back(u)
        back = wait_back(u)
        sel = collect[m, :n] + collect[m, n:]
        total = mm(sel, back).reshape(PARTS, tok, part)
        h = h_in[m].astype(F32)
        inv = inverse_rms(h)
        gain = jnp.stack([gain_ref[:, q * part : (q + 1) * part] for q in range(PARTS)])
        weighted = total * gain
        dot = jnp.sum(jnp.sum(h * weighted, axis=-1, keepdims=True), axis=0) / width
        grad = inv[None] * weighted - h * (inv * inv * inv * dot)[None]
        g_out[m] = (g_in[m].astype(F32) + grad).astype(BF16)

        @pl.when(s > 0)
        def _():
            hop(g_out, g_in, m, micro + m, s - 1).start()

        for q in range(PARTS):
            out_ref[m, :, q * part : (q + 1) * part] = g_out[m, q]
        return carry

    lax.fori_loop(0, micro, backward, 0)

    for copy in remote:
        copy.wait_send()

    def drain(u, carry):
        for buf, sem in ((send_a, a_send), (send_b, b_send)):
            view = buf.at[u, pl.ds(0, chips - 1)]
            pltpu.make_async_copy(view, view, sem.at[u]).wait()
        return carry

    lax.fori_loop(0, 2 * micro, drain, 0)
    for m in range(micro):

        @pl.when(s < sections - 1)
        def _():
            hop(h_out, h_in, m, m, s).wait_send()

        @pl.when(s > 0)
        def _():
            hop(g_out, g_in, m, micro + m, s).wait_send()


def body(tokens, norm_gain, w_gate, w_up, w_down, route_ids, route_gates):
    sections = lax.axis_size("section")
    chips = lax.axis_size("expert") // 2
    micro, tok, width = tokens.shape
    top = route_ids.shape[-1]
    half = w_gate.shape[-1]
    hidden = 2 * half
    cap = max(2, (4 * tok * top + 3 * chips - 1) // (3 * chips))
    blk = PARTS * cap
    part = width // PARTS
    groups = 4
    per = chips // groups
    grp = per * cap
    units = 2 * micro

    flat = route_ids[0].reshape(micro, tok * top)
    onehot = (flat[:, :, None] == jnp.arange(chips, dtype=jnp.int32)).astype(jnp.int32)
    before = jnp.cumsum(onehot, axis=1) - onehot
    position = jnp.sum(before * onehot, axis=-1)
    first = (flat * blk + position).reshape(micro, tok, top).transpose(0, 2, 1)
    offset = jnp.arange(PARTS, dtype=jnp.int32) * cap
    target = (first[:, :, None, :] + offset[None, None, :, None]).reshape(micro, top * PARTS * tok)
    gates = route_gates[0].transpose(0, 2, 1)
    gates = jnp.broadcast_to(gates[:, :, None, :], (micro, top, PARTS, tok)).reshape(micro, -1, 1)

    src = jnp.arange(per * blk, dtype=jnp.int32)
    dest = (src % blk // cap) * grp + src // blk * cap + src % cap
    perm_t = (dest[:, None] == src[None, :]).astype(BF16)
    perm = (src[:, None] == dest[None, :]).astype(BF16)

    dims = (sections, chips, cap, tok, width, micro, groups, half)
    vmem = pl.BlockSpec(memory_space=pltpu.VMEM)
    hbm = pl.BlockSpec(memory_space=pl.ANY)
    dma = pltpu.SemaphoreType.DMA
    result = pl.pallas_call(
        functools.partial(kernel, dims),
        out_shape=jax.ShapeDtypeStruct((micro, tok, width), BF16),
        in_specs=[vmem] * 7 + [hbm] * 3,
        out_specs=vmem,
        scratch_shapes=[
            pltpu.VMEM((width, hidden), BF16),
            pltpu.VMEM((width, hidden), BF16),
            pltpu.VMEM((hidden, width), BF16),
            pltpu.VMEM((micro, PARTS, tok, part), BF16),
            pltpu.VMEM((micro, PARTS, tok, part), BF16),
            pltpu.VMEM((micro, PARTS, tok, part), BF16),
            pltpu.VMEM((micro, PARTS, tok, part), BF16),
            pltpu.VMEM((units, chips, blk, part), BF16),
            pltpu.VMEM((units, chips, blk, part), BF16),
            pltpu.VMEM((units, chips, blk, part), BF16),
            pltpu.VMEM((units, chips, blk, part), BF16),
            pltpu.VMEM((micro, chips * blk, top * PARTS * tok), BF16),
            pltpu.VMEM((micro, top * PARTS * tok, chips * blk), BF16),
            pltpu.VMEM((top * PARTS * tok, part), BF16),
            pltpu.VMEM((groups, PARTS * grp, part), BF16),
            pltpu.VMEM((chips * cap, width), BF16),
            pltpu.VMEM((micro, hidden // 256, chips * cap, 256), F32),
            pltpu.VMEM((micro, hidden // 256, chips * cap, 256), F32),
            pltpu.VMEM((chips * cap, hidden), BF16),
            pltpu.VMEM((chips * cap, hidden), BF16),
            dma((3,)),
            dma((3,)),
            dma((3,)),
            dma((units,)),
            dma((units, groups)),
            dma((units,)),
            dma((units, groups)),
            dma((units,)),
            dma((units,)),
        ],
        compiler_params=pltpu.CompilerParams(
            collective_id=0, has_side_effects=True, vmem_limit_bytes=60 * 1024 * 1024
        ),
        name="relay",
    )(
        tokens,
        norm_gain,
        target[:, None, :],
        target[:, :, None],
        gates,
        perm,
        perm_t,
        w_gate[0],
        w_up[0],
        w_down[0],
    )
    return result[None]


def solution(mesh):
    in_specs = (
        P(None, "expert", None),
        P("section", None),
        P("section", None, "expert"),
        P("section", None, "expert"),
        P("section", "expert", None),
        P("section", None, "expert", None),
        P("section", None, "expert", None),
    )
    out_specs = P("section", None, "expert", None)
    return jax.shard_map(body, mesh=mesh, in_specs=in_specs, out_specs=out_specs, check_vma=False)
```

```python
import functools

import jax
import jax.numpy as jnp
from jax import lax
from jax.experimental import pallas as pl
from jax.experimental.pallas import tpu as pltpu
from jax.sharding import PartitionSpec as P

EPS = 1e-06
PARTS = 4
MESH = pl.DeviceIdType.MESH
F32 = jnp.float32
BF16 = jnp.bfloat16


def mm(a, b):
    return jnp.dot(a, b, preferred_element_type=F32)


def mm_nt(a, b):
    return lax.dot_general(a, b, (((1,), (1,)), ((), ())), preferred_element_type=F32)


def kernel(
    dims,
    tokens_ref,
    gain_ref,
    route_row_ref,
    route_col_ref,
    gate_col_ref,
    perm_ref,
    perm_t_ref,
    w_gate_ref,
    w_up_ref,
    w_down_ref,
    out_ref,
    wg,
    wu,
    wd,
    h_in,
    h_out,
    g_in,
    g_out,
    send_a,
    recv_a,
    send_b,
    recv_b,
    spread,
    collect,
    stage,
    pieces,
    rows,
    pre_g,
    pre_u,
    act_a,
    act_b,
    w_local,
    w_send,
    w_recv,
    a_send,
    a_recv,
    b_send,
    b_recv,
    x_send,
    x_recv,
    turn,
):
    sections, chips, cap, tok, width, micro, groups, half = dims
    blk = PARTS * cap
    part = width // PARTS
    per = chips // groups
    grp_rows = per * cap
    all_rows = chips * cap
    hidden = 2 * half
    step = 256
    s = lax.axis_index("section")
    ex = lax.axis_index("expert")
    core = lax.rem(ex, 2)
    chip = lax.div(ex, 2)
    mate = 2 * chip + (1 - core)
    my_group = lax.div(chip, per)

    leads = (s == 0) & (core == 0)

    def other(j):
        return lax.rem(chip + j, chips)

    barrier = pltpu.get_barrier_semaphore()

    def greet(j, carry):
        pl.semaphore_signal(
            barrier, inc=1, device_id={"expert": 2 * other(j) + core}, device_id_type=MESH
        )
        return carry

    lax.fori_loop(1, chips, greet, 0)
    pl.semaphore_signal(barrier, inc=1, device_id={"expert": mate}, device_id_type=MESH)

    @pl.when(s > 0)
    def _():
        pl.semaphore_signal(barrier, inc=1, device_id={"section": s - 1}, device_id_type=MESH)

    @pl.when(s < sections - 1)
    def _():
        pl.semaphore_signal(barrier, inc=1, device_id={"section": s + 1}, device_id_type=MESH)

    local = [
        pltpu.make_async_copy(w_gate_ref, wg.at[:, :half], w_local.at[0]),
        pltpu.make_async_copy(w_up_ref, wu.at[:, :half], w_local.at[1]),
        pltpu.make_async_copy(w_down_ref, wd.at[:half, :], w_local.at[2]),
    ]
    for copy in local:
        copy.start()

    ahead = lax.convert_element_type(s > 0, jnp.int32)
    behind = lax.convert_element_type(s < sections - 1, jnp.int32)
    pl.semaphore_wait(barrier, chips + ahead + behind)

    remote = [
        pltpu.make_async_remote_copy(
            src, dst, w_send.at[i], w_recv.at[i], device_id={"expert": mate}, device_id_type=MESH
        )
        for i, (src, dst) in enumerate(
            (
                (w_gate_ref, wg.at[:, half:]),
                (w_up_ref, wu.at[:, half:]),
                (w_down_ref, wd.at[half:, :]),
            )
        )
    ]
    for copy in remote:
        copy.start()

    for m in range(micro):
        for k in range(2):
            at = k * PARTS * tok
            n = PARTS * tok
            lane = route_row_ref[m, :, at : at + n]
            ids = lax.broadcasted_iota(jnp.int32, (chips * blk, n), 0)
            spread[m, :, at : at + n] = jnp.where(ids == lane, 1.0, 0.0).astype(BF16)
            sub = route_col_ref[m, at : at + n, :]
            ids = lax.broadcasted_iota(jnp.int32, (n, chips * blk), 1)
            collect[m, at : at + n, :] = jnp.where(ids == sub, 1.0, 0.0).astype(BF16)

    def send_block(u, d, src, dst, send_sem, recv_sem):
        return pltpu.make_async_remote_copy(
            src.at[u, d],
            dst.at[u, chip],
            send_sem.at[u],
            recv_sem.at[u, my_group],
            device_id={"expert": 2 * d + core},
            device_id_type=MESH,
        )

    def scatter(u, src, dst, send_sem, recv_sem):
        def one(j, carry):
            send_block(u, other(j), src, dst, send_sem, recv_sem).start()
            return carry

        lax.fori_loop(1, chips, one, 0)
        pltpu.make_async_copy(src.at[u, chip], dst.at[u, chip], recv_sem.at[u, my_group]).start()

    def sent_wait(u, buf, sem):
        view = buf.at[u, pl.ds(0, chips - 1)]
        pltpu.make_async_copy(view, view, sem.at[u]).wait()

    def group_wait(u, g, dst, recv_sem):
        view = dst.at[u, pl.ds(g * per, per)]
        pltpu.make_async_copy(view, view, recv_sem.at[u, g]).wait()

    def arrive(u):
        def one(i, carry):
            g = lax.rem(my_group + i, groups)
            group_wait(u, g, recv_a, a_recv)
            got = recv_a[u, pl.ds(g * per, per)].astype(F32).reshape(per * blk, part).astype(BF16)
            sorted_rows = mm(perm_ref[...], got).astype(BF16)
            for q in range(PARTS):
                rows[pl.ds(g * grp_rows, grp_rows), q * part : (q + 1) * part] = sorted_rows[
                    q * grp_rows : (q + 1) * grp_rows
                ]
            return carry

        lax.fori_loop(0, groups, one, 0)

    def give_back(u):
        def one(g, carry):
            got = mm(perm_t_ref[...], pieces[g])
            send_b[u, pl.ds(g * per, per)] = got.reshape(per, blk, part).astype(BF16)
            return carry

        lax.fori_loop(0, groups, one, 0)
        scatter(u, send_b, recv_b, b_send, b_recv)

    def wait_back(u):
        def one(g, carry):
            group_wait(u, g, recv_b, b_recv)
            return carry

        lax.fori_loop(0, groups, one, 0)
        return recv_b[u].astype(F32).reshape(chips * blk, part).astype(BF16)

    def put_pieces(q, value):
        for g in range(groups):
            pieces[g, pl.ds(q * grp_rows, grp_rows), :] = value[g * grp_rows : (g + 1) * grp_rows]

    def inverse_rms(h):
        total = jnp.sum(jnp.sum(h * h, axis=-1, keepdims=True), axis=0)
        return lax.rsqrt(total / width + EPS)

    def hop(buf_src, buf_dst, m, index, to):
        return pltpu.make_async_remote_copy(
            buf_src.at[m],
            buf_dst.at[m],
            x_send.at[index],
            x_recv.at[index],
            device_id={"section": to},
            device_id_type=MESH,
        )

    def forward(m, carry):
        u = m

        @pl.when(s == 0)
        def _():
            for q in range(PARTS):
                h_in[m, q] = tokens_ref[m, :, q * part : (q + 1) * part]

        @pl.when(s > 0)
        def _():
            hop(h_out, h_in, m, m, s).wait_recv()

        h = h_in[m].astype(F32)
        inv = inverse_rms(h)
        for q in range(PARTS):
            stage[pl.ds(q * tok, tok), :] = (
                h_in[m, q].astype(F32) * inv * gain_ref[:, q * part : (q + 1) * part]
            ).astype(BF16)
        n = PARTS * tok
        sel = spread[m, :, :n] + spread[m, :, n:]
        out = mm(sel, stage[:n, :])
        send_a[u] = out.reshape(chips, blk, part).astype(BF16)

        @pl.when((s == 0) & (core == 1) & (m == 0))
        def _():
            pl.semaphore_wait(turn, 1)

        scatter(u, send_a, recv_a, a_send, a_recv)

        @pl.when(leads & (m == 0))
        def _():
            sent_wait(u, send_a, a_send)
            pl.semaphore_signal(turn, inc=1, device_id={"expert": mate}, device_id_type=MESH)

        @pl.when(m == 0)
        def _():
            for copy in local:
                copy.wait()
            for copy in remote:
                copy.wait_recv()

        arrive(u)

        def first(i, carry):
            at = pl.ds(pl.multiple_of(i * step, step), step)
            gate = mm(rows[...], wg[:, at])
            up = mm(rows[...], wu[:, at])
            pre_g[m, i] = gate
            pre_u[m, i] = up
            act_a[:, at] = (gate * jax.nn.sigmoid(gate) * up).astype(BF16)
            return carry

        lax.fori_loop(0, hidden // step, first, 0)

        def second(q, carry):
            at = pl.ds(pl.multiple_of(q * part, part), part)
            put_pieces(q, mm(act_a[...], wd[:, at]).astype(BF16))
            return carry

        lax.fori_loop(0, PARTS, second, 0)
        give_back(u)
        back = wait_back(u)
        picked = mm(collect[m], back) * gate_col_ref[m]
        mixture = picked[:n] + picked[n:]
        h_out[m] = (h_in[m].astype(F32) + mixture.reshape(PARTS, tok, part)).astype(BF16)

        @pl.when(s < sections - 1)
        def _():
            hop(h_out, h_in, m, m, s + 1).start()

        return carry

    lax.fori_loop(0, micro, forward, 0)

    def backward(m, carry):
        u = micro + m

        @pl.when(s == sections - 1)
        def _():
            g_in[m] = h_out[m]

        @pl.when(s < sections - 1)
        def _():
            hop(g_out, g_in, m, micro + m, s).wait_recv()

        n = PARTS * tok
        upstream = g_in[m].astype(F32).reshape(n, part)
        stage[:n, :] = (gate_col_ref[m, :n] * upstream).astype(BF16)
        stage[n:, :] = (gate_col_ref[m, n:] * upstream).astype(BF16)
        out = mm(spread[m], stage[...])
        send_a[u] = out.reshape(chips, blk, part).astype(BF16)
        scatter(u, send_a, recv_a, a_send, a_recv)
        arrive(u)

        def first(i, carry):
            at = pl.ds(pl.multiple_of(i * step, step), step)
            grad = mm_nt(rows[...], wd[at, :])
            gate = pre_g[m, i]
            up = pre_u[m, i]
            logistic = jax.nn.sigmoid(gate)
            act_a[:, at] = (grad * up * logistic * (1.0 + gate * (1.0 - logistic))).astype(BF16)
            act_b[:, at] = (grad * gate * logistic).astype(BF16)
            return carry

        lax.fori_loop(0, hidden // step, first, 0)

        def second(q, carry):
            at = pl.ds(pl.multiple_of(q * part, part), part)
            value = mm_nt(act_a[...], wg[at, :]) + mm_nt(act_b[...], wu[at, :])
            put_pieces(q, value.astype(BF16))
            return carry

        lax.fori_loop(0, PARTS, second, 0)
        give_back(u)
        back = wait_back(u)
        sel = collect[m, :n] + collect[m, n:]
        total = mm(sel, back).reshape(PARTS, tok, part)
        h = h_in[m].astype(F32)
        inv = inverse_rms(h)
        gain = jnp.stack([gain_ref[:, q * part : (q + 1) * part] for q in range(PARTS)])
        weighted = total * gain
        dot = jnp.sum(jnp.sum(h * weighted, axis=-1, keepdims=True), axis=0) / width
        grad = inv[None] * weighted - h * (inv * inv * inv * dot)[None]
        g_out[m] = (g_in[m].astype(F32) + grad).astype(BF16)

        @pl.when(s > 0)
        def _():
            hop(g_out, g_in, m, micro + m, s - 1).start()

        for q in range(PARTS):
            out_ref[m, :, q * part : (q + 1) * part] = g_out[m, q]
        return carry

    lax.fori_loop(0, micro, backward, 0)

    for copy in remote:
        copy.wait_send()

    def drain(u, carry):
        @pl.when(jnp.logical_not(leads & (u == 0)))
        def _():
            sent_wait(u, send_a, a_send)

        sent_wait(u, send_b, b_send)
        return carry

    lax.fori_loop(0, 2 * micro, drain, 0)
    for m in range(micro):

        @pl.when(s < sections - 1)
        def _():
            hop(h_out, h_in, m, m, s).wait_send()

        @pl.when(s > 0)
        def _():
            hop(g_out, g_in, m, micro + m, s).wait_send()


def body(tokens, norm_gain, w_gate, w_up, w_down, route_ids, route_gates):
    sections = lax.axis_size("section")
    chips = lax.axis_size("expert") // 2
    micro, tok, width = tokens.shape
    top = route_ids.shape[-1]
    half = w_gate.shape[-1]
    hidden = 2 * half
    cap = max(2, (4 * tok * top + 3 * chips - 1) // (3 * chips))
    blk = PARTS * cap
    part = width // PARTS
    groups = 4
    per = chips // groups
    grp = per * cap
    units = 2 * micro

    flat = route_ids[0].reshape(micro, tok * top)
    onehot = (flat[:, :, None] == jnp.arange(chips, dtype=jnp.int32)).astype(jnp.int32)
    before = jnp.cumsum(onehot, axis=1) - onehot
    position = jnp.sum(before * onehot, axis=-1)
    first = (flat * blk + position).reshape(micro, tok, top).transpose(0, 2, 1)
    offset = jnp.arange(PARTS, dtype=jnp.int32) * cap
    target = (first[:, :, None, :] + offset[None, None, :, None]).reshape(micro, top * PARTS * tok)
    gates = route_gates[0].transpose(0, 2, 1)
    gates = jnp.broadcast_to(gates[:, :, None, :], (micro, top, PARTS, tok)).reshape(micro, -1, 1)

    src = jnp.arange(per * blk, dtype=jnp.int32)
    dest = (src % blk // cap) * grp + src // blk * cap + src % cap
    perm_t = (dest[:, None] == src[None, :]).astype(BF16)
    perm = (src[:, None] == dest[None, :]).astype(BF16)

    dims = (sections, chips, cap, tok, width, micro, groups, half)
    vmem = pl.BlockSpec(memory_space=pltpu.VMEM)
    hbm = pl.BlockSpec(memory_space=pl.ANY)
    dma = pltpu.SemaphoreType.DMA
    result = pl.pallas_call(
        functools.partial(kernel, dims),
        out_shape=jax.ShapeDtypeStruct((micro, tok, width), BF16),
        in_specs=[vmem] * 7 + [hbm] * 3,
        out_specs=vmem,
        scratch_shapes=[
            pltpu.VMEM((width, hidden), BF16),
            pltpu.VMEM((width, hidden), BF16),
            pltpu.VMEM((hidden, width), BF16),
            pltpu.VMEM((micro, PARTS, tok, part), BF16),
            pltpu.VMEM((micro, PARTS, tok, part), BF16),
            pltpu.VMEM((micro, PARTS, tok, part), BF16),
            pltpu.VMEM((micro, PARTS, tok, part), BF16),
            pltpu.VMEM((units, chips, blk, part), BF16),
            pltpu.VMEM((units, chips, blk, part), BF16),
            pltpu.VMEM((units, chips, blk, part), BF16),
            pltpu.VMEM((units, chips, blk, part), BF16),
            pltpu.VMEM((micro, chips * blk, top * PARTS * tok), BF16),
            pltpu.VMEM((micro, top * PARTS * tok, chips * blk), BF16),
            pltpu.VMEM((top * PARTS * tok, part), BF16),
            pltpu.VMEM((groups, PARTS * grp, part), BF16),
            pltpu.VMEM((chips * cap, width), BF16),
            pltpu.VMEM((micro, hidden // 256, chips * cap, 256), F32),
            pltpu.VMEM((micro, hidden // 256, chips * cap, 256), F32),
            pltpu.VMEM((chips * cap, hidden), BF16),
            pltpu.VMEM((chips * cap, hidden), BF16),
            dma((3,)),
            dma((3,)),
            dma((3,)),
            dma((units,)),
            dma((units, groups)),
            dma((units,)),
            dma((units, groups)),
            dma((units,)),
            dma((units,)),
            pltpu.SemaphoreType.REGULAR,
        ],
        compiler_params=pltpu.CompilerParams(
            collective_id=0, has_side_effects=True, vmem_limit_bytes=60 * 1024 * 1024
        ),
        name="relay",
    )(
        tokens,
        norm_gain,
        target[:, None, :],
        target[:, :, None],
        gates,
        perm,
        perm_t,
        w_gate[0],
        w_up[0],
        w_down[0],
    )
    return result[None]


def solution(mesh):
    in_specs = (
        P(None, "expert", None),
        P("section", None),
        P("section", None, "expert"),
        P("section", None, "expert"),
        P("section", "expert", None),
        P("section", None, "expert", None),
        P("section", None, "expert", None),
    )
    out_specs = P("section", None, "expert", None)
    return jax.shard_map(body, mesh=mesh, in_specs=in_specs, out_specs=out_specs, check_vma=False)
```

```python
import functools

import jax
import jax.numpy as jnp
from jax import lax
from jax.experimental import pallas as pl
from jax.experimental.pallas import tpu as pltpu
from jax.sharding import PartitionSpec as P

EPS = 1e-06
PARTS = 4
MESH = pl.DeviceIdType.MESH
F32 = jnp.float32
BF16 = jnp.bfloat16


def mm(a, b):
    return jnp.dot(a, b, preferred_element_type=F32)


def mm_nt(a, b):
    return lax.dot_general(a, b, (((1,), (1,)), ((), ())), preferred_element_type=F32)


def kernel(
    dims,
    tokens_ref,
    gain_ref,
    route_row_ref,
    route_col_ref,
    gate_col_ref,
    perm_ref,
    perm_t_ref,
    w_gate_ref,
    w_up_ref,
    w_down_ref,
    out_ref,
    wg,
    wu,
    wd,
    h_in,
    h_out,
    g_in,
    g_out,
    send_a,
    recv_a,
    send_b,
    recv_b,
    spread,
    collect,
    stage,
    pieces,
    rows,
    pre_g,
    pre_u,
    act_a,
    act_b,
    w_local,
    w_send,
    w_recv,
    a_send,
    a_recv,
    b_send,
    b_recv,
    x_send,
    x_recv,
    turn,
):
    sections, chips, cap, tok, width, micro, groups, half = dims
    blk = PARTS * cap
    part = width // PARTS
    per = chips // groups
    grp_rows = per * cap
    all_rows = chips * cap
    hidden = 2 * half
    step = 256
    mark = 2
    s = lax.axis_index("section")
    ex = lax.axis_index("expert")
    core = lax.rem(ex, 2)
    chip = lax.div(ex, 2)
    mate = 2 * chip + (1 - core)
    my_group = lax.div(chip, per)

    def other(j):
        g = lax.rem(my_group + lax.div(j, per), groups)
        return g * per + lax.rem(chip + j, per)

    barrier = pltpu.get_barrier_semaphore()

    def greet(j, carry):
        pl.semaphore_signal(
            barrier, inc=1, device_id={"expert": 2 * other(j) + core}, device_id_type=MESH
        )
        return carry

    lax.fori_loop(1, chips, greet, 0)
    pl.semaphore_signal(barrier, inc=1, device_id={"expert": mate}, device_id_type=MESH)

    @pl.when(s > 0)
    def _():
        pl.semaphore_signal(barrier, inc=1, device_id={"section": s - 1}, device_id_type=MESH)

    @pl.when(s < sections - 1)
    def _():
        pl.semaphore_signal(barrier, inc=1, device_id={"section": s + 1}, device_id_type=MESH)

    local = [
        pltpu.make_async_copy(w_gate_ref, wg.at[:, :half], w_local.at[0]),
        pltpu.make_async_copy(w_up_ref, wu.at[:, :half], w_local.at[1]),
        pltpu.make_async_copy(w_down_ref, wd.at[:half, :], w_local.at[2]),
    ]
    for copy in local:
        copy.start()

    ahead = lax.convert_element_type(s > 0, jnp.int32)
    behind = lax.convert_element_type(s < sections - 1, jnp.int32)
    pl.semaphore_wait(barrier, chips + ahead + behind)

    remote = [
        pltpu.make_async_remote_copy(
            src, dst, w_send.at[i], w_recv.at[i], device_id={"expert": mate}, device_id_type=MESH
        )
        for i, (src, dst) in enumerate(
            (
                (w_gate_ref, wg.at[:, half:]),
                (w_up_ref, wu.at[:, half:]),
                (w_down_ref, wd.at[half:, :]),
            )
        )
    ]
    for copy in remote:
        copy.start()

    for m in range(micro):
        for k in range(2):
            at = k * PARTS * tok
            n = PARTS * tok
            lane = route_row_ref[m, :, at : at + n]
            ids = lax.broadcasted_iota(jnp.int32, (chips * blk, n), 0)
            spread[m, :, at : at + n] = jnp.where(ids == lane, 1.0, 0.0).astype(BF16)
            sub = route_col_ref[m, at : at + n, :]
            ids = lax.broadcasted_iota(jnp.int32, (n, chips * blk), 1)
            collect[m, at : at + n, :] = jnp.where(ids == sub, 1.0, 0.0).astype(BF16)

    def send_block(u, d, src, dst, send_sem, recv_sem):
        return pltpu.make_async_remote_copy(
            src.at[u, d],
            dst.at[u, chip],
            send_sem.at[u],
            recv_sem.at[u, my_group],
            device_id={"expert": 2 * d + core},
            device_id_type=MESH,
        )

    def scatter(u, src, dst, send_sem, recv_sem):
        @pl.when(core == 1)
        def _():
            pl.semaphore_wait(turn, 1)

        def one(j, carry):
            send_block(u, other(j), src, dst, send_sem, recv_sem).start()
            return carry

        lax.fori_loop(1, chips, one, 0)
        pltpu.make_async_copy(src.at[u, chip], dst.at[u, chip], recv_sem.at[u, my_group]).start()

    def sent_wait(u, buf, sem):
        view = buf.at[u, pl.ds(0, chips - 1)]
        pltpu.make_async_copy(view, view, sem.at[u]).wait()

    def group_wait(u, i, dst, recv_sem):
        g = lax.rem(my_group + groups - i, groups)
        view = dst.at[u, pl.ds(g * per, per)]
        pltpu.make_async_copy(view, view, recv_sem.at[u, g]).wait()

        @pl.when((core == 0) & (i == mark))
        def _():
            pl.semaphore_signal(turn, inc=1, device_id={"expert": mate}, device_id_type=MESH)

        return g

    def arrive(u):
        def one(i, carry):
            g = group_wait(u, i, recv_a, a_recv)
            got = recv_a[u, pl.ds(g * per, per)].astype(F32).reshape(per * blk, part).astype(BF16)
            sorted_rows = mm(perm_ref[...], got).astype(BF16)
            for q in range(PARTS):
                rows[pl.ds(g * grp_rows, grp_rows), q * part : (q + 1) * part] = sorted_rows[
                    q * grp_rows : (q + 1) * grp_rows
                ]
            return carry

        lax.fori_loop(0, groups, one, 0)

    def give_back(u):
        def one(g, carry):
            got = mm(perm_t_ref[...], pieces[g])
            send_b[u, pl.ds(g * per, per)] = got.reshape(per, blk, part).astype(BF16)
            return carry

        lax.fori_loop(0, groups, one, 0)
        scatter(u, send_b, recv_b, b_send, b_recv)

    def wait_back(u):
        def one(i, carry):
            group_wait(u, i, recv_b, b_recv)
            return carry

        lax.fori_loop(0, groups, one, 0)
        return recv_b[u].astype(F32).reshape(chips * blk, part).astype(BF16)

    def put_pieces(q, value):
        for g in range(groups):
            pieces[g, pl.ds(q * grp_rows, grp_rows), :] = value[g * grp_rows : (g + 1) * grp_rows]

    def inverse_rms(h):
        total = jnp.sum(jnp.sum(h * h, axis=-1, keepdims=True), axis=0)
        return lax.rsqrt(total / width + EPS)

    def hop(buf_src, buf_dst, m, index, to):
        return pltpu.make_async_remote_copy(
            buf_src.at[m],
            buf_dst.at[m],
            x_send.at[index],
            x_recv.at[index],
            device_id={"section": to},
            device_id_type=MESH,
        )

    def forward(m, carry):
        u = m

        @pl.when(s == 0)
        def _():
            for q in range(PARTS):
                h_in[m, q] = tokens_ref[m, :, q * part : (q + 1) * part]

        @pl.when(s > 0)
        def _():
            hop(h_out, h_in, m, m, s).wait_recv()

        h = h_in[m].astype(F32)
        inv = inverse_rms(h)
        for q in range(PARTS):
            stage[pl.ds(q * tok, tok), :] = (
                h_in[m, q].astype(F32) * inv * gain_ref[:, q * part : (q + 1) * part]
            ).astype(BF16)
        n = PARTS * tok
        sel = spread[m, :, :n] + spread[m, :, n:]
        out = mm(sel, stage[:n, :])
        send_a[u] = out.reshape(chips, blk, part).astype(BF16)

        scatter(u, send_a, recv_a, a_send, a_recv)

        @pl.when(m == 0)
        def _():
            for copy in local:
                copy.wait()
            for copy in remote:
                copy.wait_recv()

        arrive(u)

        def first(i, carry):
            at = pl.ds(pl.multiple_of(i * step, step), step)
            gate = mm(rows[...], wg[:, at])
            up = mm(rows[...], wu[:, at])
            pre_g[m, i] = gate
            pre_u[m, i] = up
            act_a[:, at] = (gate * jax.nn.sigmoid(gate) * up).astype(BF16)
            return carry

        lax.fori_loop(0, hidden // step, first, 0)

        def second(q, carry):
            at = pl.ds(pl.multiple_of(q * part, part), part)
            put_pieces(q, mm(act_a[...], wd[:, at]).astype(BF16))
            return carry

        lax.fori_loop(0, PARTS, second, 0)
        give_back(u)
        back = wait_back(u)
        picked = mm(collect[m], back) * gate_col_ref[m]
        mixture = picked[:n] + picked[n:]
        h_out[m] = (h_in[m].astype(F32) + mixture.reshape(PARTS, tok, part)).astype(BF16)

        @pl.when(s < sections - 1)
        def _():
            hop(h_out, h_in, m, m, s + 1).start()

        return carry

    lax.fori_loop(0, micro, forward, 0)

    def backward(m, carry):
        u = micro + m

        @pl.when(s == sections - 1)
        def _():
            g_in[m] = h_out[m]

        @pl.when(s < sections - 1)
        def _():
            hop(g_out, g_in, m, micro + m, s).wait_recv()

        n = PARTS * tok
        upstream = g_in[m].astype(F32).reshape(n, part)
        stage[:n, :] = (gate_col_ref[m, :n] * upstream).astype(BF16)
        stage[n:, :] = (gate_col_ref[m, n:] * upstream).astype(BF16)
        out = mm(spread[m], stage[...])
        send_a[u] = out.reshape(chips, blk, part).astype(BF16)
        scatter(u, send_a, recv_a, a_send, a_recv)
        arrive(u)

        def first(i, carry):
            at = pl.ds(pl.multiple_of(i * step, step), step)
            grad = mm_nt(rows[...], wd[at, :])
            gate = pre_g[m, i]
            up = pre_u[m, i]
            logistic = jax.nn.sigmoid(gate)
            act_a[:, at] = (grad * up * logistic * (1.0 + gate * (1.0 - logistic))).astype(BF16)
            act_b[:, at] = (grad * gate * logistic).astype(BF16)
            return carry

        lax.fori_loop(0, hidden // step, first, 0)

        def second(q, carry):
            at = pl.ds(pl.multiple_of(q * part, part), part)
            value = mm_nt(act_a[...], wg[at, :]) + mm_nt(act_b[...], wu[at, :])
            put_pieces(q, value.astype(BF16))
            return carry

        lax.fori_loop(0, PARTS, second, 0)
        give_back(u)
        back = wait_back(u)
        sel = collect[m, :n] + collect[m, n:]
        total = mm(sel, back).reshape(PARTS, tok, part)
        h = h_in[m].astype(F32)
        inv = inverse_rms(h)
        gain = jnp.stack([gain_ref[:, q * part : (q + 1) * part] for q in range(PARTS)])
        weighted = total * gain
        dot = jnp.sum(jnp.sum(h * weighted, axis=-1, keepdims=True), axis=0) / width
        grad = inv[None] * weighted - h * (inv * inv * inv * dot)[None]
        g_out[m] = (g_in[m].astype(F32) + grad).astype(BF16)

        @pl.when(s > 0)
        def _():
            hop(g_out, g_in, m, micro + m, s - 1).start()

        for q in range(PARTS):
            out_ref[m, :, q * part : (q + 1) * part] = g_out[m, q]
        return carry

    lax.fori_loop(0, micro, backward, 0)

    for copy in remote:
        copy.wait_send()

    def drain(u, carry):
        sent_wait(u, send_a, a_send)
        sent_wait(u, send_b, b_send)
        return carry

    lax.fori_loop(0, 2 * micro, drain, 0)
    for m in range(micro):

        @pl.when(s < sections - 1)
        def _():
            hop(h_out, h_in, m, m, s).wait_send()

        @pl.when(s > 0)
        def _():
            hop(g_out, g_in, m, micro + m, s).wait_send()


def body(tokens, norm_gain, w_gate, w_up, w_down, route_ids, route_gates):
    sections = lax.axis_size("section")
    chips = lax.axis_size("expert") // 2
    micro, tok, width = tokens.shape
    top = route_ids.shape[-1]
    half = w_gate.shape[-1]
    hidden = 2 * half
    cap = max(2, (4 * tok * top + 3 * chips - 1) // (3 * chips))
    blk = PARTS * cap
    part = width // PARTS
    groups = 4
    per = chips // groups
    grp = per * cap
    units = 2 * micro

    flat = route_ids[0].reshape(micro, tok * top)
    onehot = (flat[:, :, None] == jnp.arange(chips, dtype=jnp.int32)).astype(jnp.int32)
    before = jnp.cumsum(onehot, axis=1) - onehot
    position = jnp.sum(before * onehot, axis=-1)
    first = (flat * blk + position).reshape(micro, tok, top).transpose(0, 2, 1)
    offset = jnp.arange(PARTS, dtype=jnp.int32) * cap
    target = (first[:, :, None, :] + offset[None, None, :, None]).reshape(micro, top * PARTS * tok)
    gates = route_gates[0].transpose(0, 2, 1)
    gates = jnp.broadcast_to(gates[:, :, None, :], (micro, top, PARTS, tok)).reshape(micro, -1, 1)

    src = jnp.arange(per * blk, dtype=jnp.int32)
    dest = (src % blk // cap) * grp + src // blk * cap + src % cap
    perm_t = (dest[:, None] == src[None, :]).astype(BF16)
    perm = (src[:, None] == dest[None, :]).astype(BF16)

    dims = (sections, chips, cap, tok, width, micro, groups, half)
    vmem = pl.BlockSpec(memory_space=pltpu.VMEM)
    hbm = pl.BlockSpec(memory_space=pl.ANY)
    dma = pltpu.SemaphoreType.DMA
    result = pl.pallas_call(
        functools.partial(kernel, dims),
        out_shape=jax.ShapeDtypeStruct((micro, tok, width), BF16),
        in_specs=[vmem] * 7 + [hbm] * 3,
        out_specs=vmem,
        scratch_shapes=[
            pltpu.VMEM((width, hidden), BF16),
            pltpu.VMEM((width, hidden), BF16),
            pltpu.VMEM((hidden, width), BF16),
            pltpu.VMEM((micro, PARTS, tok, part), BF16),
            pltpu.VMEM((micro, PARTS, tok, part), BF16),
            pltpu.VMEM((micro, PARTS, tok, part), BF16),
            pltpu.VMEM((micro, PARTS, tok, part), BF16),
            pltpu.VMEM((units, chips, blk, part), BF16),
            pltpu.VMEM((units, chips, blk, part), BF16),
            pltpu.VMEM((units, chips, blk, part), BF16),
            pltpu.VMEM((units, chips, blk, part), BF16),
            pltpu.VMEM((micro, chips * blk, top * PARTS * tok), BF16),
            pltpu.VMEM((micro, top * PARTS * tok, chips * blk), BF16),
            pltpu.VMEM((top * PARTS * tok, part), BF16),
            pltpu.VMEM((groups, PARTS * grp, part), BF16),
            pltpu.VMEM((chips * cap, width), BF16),
            pltpu.VMEM((micro, hidden // 256, chips * cap, 256), F32),
            pltpu.VMEM((micro, hidden // 256, chips * cap, 256), F32),
            pltpu.VMEM((chips * cap, hidden), BF16),
            pltpu.VMEM((chips * cap, hidden), BF16),
            dma((3,)),
            dma((3,)),
            dma((3,)),
            dma((units,)),
            dma((units, groups)),
            dma((units,)),
            dma((units, groups)),
            dma((units,)),
            dma((units,)),
            pltpu.SemaphoreType.REGULAR,
        ],
        compiler_params=pltpu.CompilerParams(
            collective_id=0, has_side_effects=True, vmem_limit_bytes=60 * 1024 * 1024
        ),
        name="relay",
    )(
        tokens,
        norm_gain,
        target[:, None, :],
        target[:, :, None],
        gates,
        perm,
        perm_t,
        w_gate[0],
        w_up[0],
        w_down[0],
    )
    return result[None]


def solution(mesh):
    in_specs = (
        P(None, "expert", None),
        P("section", None),
        P("section", None, "expert"),
        P("section", None, "expert"),
        P("section", "expert", None),
        P("section", None, "expert", None),
        P("section", None, "expert", None),
    )
    out_specs = P("section", None, "expert", None)
    return jax.shard_map(body, mesh=mesh, in_specs=in_specs, out_specs=out_specs, check_vma=False)
```

```python
import functools

import jax
import jax.numpy as jnp
from jax import lax
from jax.experimental import pallas as pl
from jax.experimental.pallas import tpu as pltpu
from jax.sharding import PartitionSpec as P

EPS = 1e-06
PARTS = 4
MESH = pl.DeviceIdType.MESH
F32 = jnp.float32
BF16 = jnp.bfloat16


def mm(a, b):
    return jnp.dot(a, b, preferred_element_type=F32)


def mm_nt(a, b):
    return lax.dot_general(a, b, (((1,), (1,)), ((), ())), preferred_element_type=F32)


def kernel(
    dims,
    tokens_ref,
    info_ref,
    perm_ref,
    perm_t_ref,
    w_gate_ref,
    w_up_ref,
    w_down_ref,
    out_ref,
    wg,
    wu,
    wd,
    info_near,
    cols,
    h_in,
    h_prev,
    h_next,
    g_in,
    g_next,
    o_in,
    send_a,
    recv_a,
    send_b,
    recv_b,
    spread,
    collect,
    stage,
    pieces,
    rows,
    pre_g,
    pre_u,
    act_a,
    act_b,
    w_local,
    w_send,
    w_recv,
    i_send,
    i_recv,
    a_send,
    a_recv,
    b_send,
    b_recv,
    x_send,
    x_recv,
    turn,
):
    sections, chips, cap, tok, width, micro, groups, half = dims
    blk = PARTS * cap
    part = width // PARTS
    per = chips // groups
    grp_rows = per * cap
    hidden = 2 * half
    n = PARTS * tok
    step = 256
    mark = 1
    last = sections - 1
    prev, own, after = 0, 1, 2
    s = lax.axis_index("section")
    ex = lax.axis_index("expert")
    core = lax.rem(ex, 2)
    chip = lax.div(ex, 2)
    mate = 2 * chip + (1 - core)
    my_group = lax.div(chip, per)

    def other(j):
        g = lax.rem(my_group + lax.div(j, per), groups)
        return g * per + lax.rem(chip + j, per)

    barrier = pltpu.get_barrier_semaphore()

    def greet(section, j):
        pl.semaphore_signal(
            barrier,
            inc=1,
            device_id={"section": section, "expert": 2 * other(j) + core},
            device_id_type=MESH,
        )

    def greet_own(j, carry):
        greet(s, j)
        return carry

    lax.fori_loop(1, chips, greet_own, 0)
    pl.semaphore_signal(barrier, inc=1, device_id={"expert": mate}, device_id_type=MESH)

    @pl.when(s > 0)
    def _():
        def one(j, carry):
            greet(s - 1, j)
            return carry

        lax.fori_loop(0, chips, one, 0)

    @pl.when(s < last)
    def _():
        def one(j, carry):
            greet(s + 1, j)
            return carry

        lax.fori_loop(0, chips, one, 0)

    local = [
        pltpu.make_async_copy(w_gate_ref, wg.at[:, :half], w_local.at[0]),
        pltpu.make_async_copy(w_up_ref, wu.at[:, :half], w_local.at[1]),
        pltpu.make_async_copy(w_down_ref, wd.at[:half, :], w_local.at[2]),
    ]
    for copy in local:
        copy.start()

    def columns(which, ref):
        cols[which] = jnp.transpose(ref[:, : 2 * n])

    def build(which, m):
        for k in range(2):
            at = k * n
            sub = cols[which, at : at + n, :][:, m : m + 1]
            ids = lax.broadcasted_iota(jnp.int32, (n, chips * blk), 1)
            collect[which, m, at : at + n, :] = jnp.where(
                ids == sub.astype(jnp.int32), 1.0, 0.0
            ).astype(BF16)

    for m in range(micro):
        for k in range(2):
            at = k * n
            lane = info_ref[m : m + 1, at : at + n].astype(jnp.int32)
            ids = lax.broadcasted_iota(jnp.int32, (chips * blk, n), 0)
            spread[m, :, at : at + n] = jnp.where(ids == lane, 1.0, 0.0).astype(BF16)

    ahead = lax.convert_element_type(s > 0, jnp.int32)
    behind = lax.convert_element_type(s < last, jnp.int32)
    pl.semaphore_wait(barrier, chips + chips * ahead + chips * behind)

    remote = [
        pltpu.make_async_remote_copy(
            src, dst, w_send.at[i], w_recv.at[i], device_id={"expert": mate}, device_id_type=MESH
        )
        for i, (src, dst) in enumerate(
            (
                (w_gate_ref, wg.at[:, half:]),
                (w_up_ref, wu.at[:, half:]),
                (w_down_ref, wd.at[half:, :]),
            )
        )
    ]
    for copy in remote:
        copy.start()

    def tell(slot, to):
        return pltpu.make_async_remote_copy(
            info_ref,
            info_near.at[slot],
            i_send.at[slot],
            i_recv.at[slot],
            device_id={"section": to},
            device_id_type=MESH,
        )

    @pl.when(s < last)
    def _():
        tell(0, s + 1).start()

    @pl.when(s > 0)
    def _():
        tell(1, s - 1).start()

    def hop(src, dst, m, kind, to):
        return pltpu.make_async_remote_copy(
            src.at[m],
            dst.at[m],
            x_send.at[kind, m],
            x_recv.at[kind, m],
            device_id={"section": to},
            device_id_type=MESH,
        )

    h_on = functools.partial(hop, h_in, h_prev, kind=0)
    h_back = functools.partial(hop, h_in, h_next, kind=1)
    g_back = functools.partial(hop, g_in, g_next, kind=2)
    o_on = functools.partial(hop, g_in, o_in, kind=3)

    def send_wait(buf, u, sem, count):
        view = buf.at[u, pl.ds(0, count)]
        pltpu.make_async_copy(view, view, sem.at[u]).wait()

    def group_wait(buf, u, i, sem):
        g = lax.rem(my_group + groups - i, groups)
        view = buf.at[u, pl.ds(g * per, per)]
        pltpu.make_async_copy(view, view, sem.at[u, g]).wait()
        return g

    def dispatch(u, m):
        send_a[u] = mm(
            spread[m] if stage_full[0] else spread[m, :, :n] + spread[m, :, n:],
            stage[...] if stage_full[0] else stage[:n, :],
        ).reshape(chips, blk, part).astype(BF16)

        @pl.when(core == 1)
        def _():
            pl.semaphore_wait(turn, 1)

        def one(j, carry):
            d = other(j)
            pltpu.make_async_remote_copy(
                send_a.at[u, d],
                recv_a.at[u, chip],
                a_send.at[u],
                a_recv.at[u, my_group],
                device_id={"expert": 2 * d + core},
                device_id_type=MESH,
            ).start()
            return carry

        lax.fori_loop(1, chips, one, 0)
        pltpu.make_async_copy(send_a.at[u, chip], recv_a.at[u, chip], a_recv.at[u, my_group]).start()

    def arrive(u):
        def one(i, carry):
            g = group_wait(recv_a, u, i, a_recv)

            @pl.when((core == 0) & (i == mark))
            def _():
                pl.semaphore_signal(turn, inc=1, device_id={"expert": mate}, device_id_type=MESH)

            got = recv_a[u, pl.ds(g * per, per)].astype(F32).reshape(per * blk, part).astype(BF16)
            sorted_rows = mm(perm_ref[...], got).astype(BF16)
            for q in range(PARTS):
                rows[pl.ds(g * grp_rows, grp_rows), q * part : (q + 1) * part] = sorted_rows[
                    q * grp_rows : (q + 1) * grp_rows
                ]
            return carry

        lax.fori_loop(0, groups, one, 0)

    def give_back(u, to, slot):
        def one(i, carry):
            g = lax.rem(my_group + i, groups)
            got = mm(perm_t_ref[...], pieces[g])
            send_b[u, pl.ds(g * per, per)] = got.reshape(per, blk, part).astype(BF16)

            def block(j, inner):
                d = g * per + lax.rem(chip + j, per)

                @pl.when(jnp.logical_or(d != chip, to != s))
                def _():
                    pltpu.make_async_remote_copy(
                        send_b.at[u, d],
                        recv_b.at[slot, chip],
                        b_send.at[u],
                        b_recv.at[slot, my_group],
                        device_id={"section": to, "expert": 2 * d + core},
                        device_id_type=MESH,
                    ).start()

                return inner

            return lax.fori_loop(0, per, block, carry)

        lax.fori_loop(0, groups, one, 0)

        @pl.when(to == s)
        def _():
            pltpu.make_async_copy(
                send_b.at[u, chip], recv_b.at[slot, chip], b_recv.at[slot, my_group]
            ).start()

    def wait_back(slot):
        def one(i, carry):
            group_wait(recv_b, slot, i, b_recv)
            return carry

        lax.fori_loop(0, groups, one, 0)
        return recv_b[slot].astype(F32).reshape(chips * blk, part).astype(BF16)

    def put_pieces(q, value):
        for g in range(groups):
            pieces[g, pl.ds(q * grp_rows, grp_rows), :] = value[g * grp_rows : (g + 1) * grp_rows]

    def gate_column(which, m):
        return jnp.where(m == 0, cols[which][:, micro : micro + 1], cols[which][:, micro + 1 : micro + 2])

    def inverse_rms(h):
        total = jnp.sum(jnp.sum(h * h, axis=-1, keepdims=True), axis=0)
        return lax.rsqrt(total / width + EPS)

    def mix(h, slot, which, m):
        picked = mm(collect[which, m], wait_back(slot)) * gate_column(which, m)
        mixture = picked[:n] + picked[n:]
        return (h.astype(F32) + mixture.reshape(PARTS, tok, part)).astype(BF16)

    def grad(g, h, gain, slot, which, m):
        sel = collect[which, m, :n] + collect[which, m, n:]
        total = mm(sel, wait_back(slot)).reshape(PARTS, tok, part)
        h = h.astype(F32)
        inv = inverse_rms(h)
        weighted = total * jnp.stack([gain[2 * micro + q : 2 * micro + q + 1, :] for q in range(PARTS)])
        dot = jnp.sum(jnp.sum(h * weighted, axis=-1, keepdims=True), axis=0) / width
        change = inv[None] * weighted - h * (inv * inv * inv * dot)[None]
        return (g.astype(F32) + change).astype(BF16)

    columns(own, info_ref)
    stage_full = [False]

    @pl.when(s > 0)
    def _():
        tell(0, s).wait_recv()
        columns(prev, info_near.at[0])
        for m in range(micro):
            build(prev, m)

    def forward(m, carry):
        u = m

        @pl.when(s == 0)
        def _():
            for q in range(PARTS):
                h_in[m, q] = tokens_ref[m, :, q * part : (q + 1) * part]

        @pl.when(s > 0)
        def _():
            h_on(m=m, to=s).wait_recv()
            h_in[m] = mix(h_prev[m], m, prev, m)

        inv = inverse_rms(h_in[m].astype(F32))
        for q in range(PARTS):
            gain = info_ref[2 * micro + q : 2 * micro + q + 1, :]
            stage[pl.ds(q * tok, tok), :] = (h_in[m, q].astype(F32) * inv * gain).astype(BF16)
        dispatch(u, m)

        @pl.when(s < last)
        def _():
            h_on(m=m, to=s + 1).start()

        @pl.when(s > 0)
        def _():
            h_back(m=m, to=s - 1).start()

        @pl.when(m == 0)
        def _():
            for copy in local:
                copy.wait()
            for copy in remote:
                copy.wait_recv()
            for i in range(micro):
                build(own, i)

            @pl.when(s < last)
            def _():
                tell(1, s).wait_recv()
                columns(after, info_near.at[1])
                for i in range(micro):
                    build(after, i)

        arrive(u)

        def first(i, carry):
            at = pl.ds(pl.multiple_of(i * step, step), step)
            gate = mm(rows[...], wg[:, at])
            up = mm(rows[...], wu[:, at])
            pre_g[m, i] = gate
            pre_u[m, i] = up
            act_a[:, at] = (gate * jax.nn.sigmoid(gate) * up).astype(BF16)
            return carry

        lax.fori_loop(0, hidden // step, first, 0)

        def second(q, carry):
            at = pl.ds(pl.multiple_of(q * part, part), part)
            put_pieces(q, mm(act_a[...], wd[:, at]).astype(BF16))
            return carry

        lax.fori_loop(0, PARTS, second, 0)
        give_back(u, jnp.minimum(s + 1, last), m + micro * (1 - behind))

        @pl.when(s == last)
        def _():
            g_in[m] = mix(h_in[m], micro + m, own, m)

        return carry

    lax.fori_loop(0, micro, forward, 0)
    stage_full[0] = True

    def backward(m, carry):
        u = micro + m

        @pl.when(s < last)
        def _():
            g_back(m=m, to=s).wait_recv()
            h_back(m=m, to=s).wait_recv()
            g_in[m] = grad(g_next[m], h_next[m], info_near.at[1], 2 * micro + m, after, m)

        upstream = g_in[m].astype(F32).reshape(n, part)
        gates = gate_column(own, m)
        stage[:n, :] = (gates[:n] * upstream).astype(BF16)
        stage[n:, :] = (gates[n:] * upstream).astype(BF16)
        dispatch(u, m)

        @pl.when(s > 0)
        def _():
            g_back(m=m, to=s - 1).start()

        @pl.when(s < last)
        def _():
            o_on(m=m, to=s + 1).start()

        arrive(u)

        def first(i, carry):
            at = pl.ds(pl.multiple_of(i * step, step), step)
            grad_hidden = mm_nt(rows[...], wd[at, :])
            gate = pre_g[m, i]
            up = pre_u[m, i]
            logistic = jax.nn.sigmoid(gate)
            act_a[:, at] = (grad_hidden * up * logistic * (1.0 + gate * (1.0 - logistic))).astype(BF16)
            act_b[:, at] = (grad_hidden * gate * logistic).astype(BF16)
            return carry

        lax.fori_loop(0, hidden // step, first, 0)

        def second(q, carry):
            at = pl.ds(pl.multiple_of(q * part, part), part)
            value = mm_nt(act_a[...], wg[at, :]) + mm_nt(act_b[...], wu[at, :])
            put_pieces(q, value.astype(BF16))
            return carry

        lax.fori_loop(0, PARTS, second, 0)
        give_back(u, jnp.maximum(s - 1, 0), 2 * micro + m + micro * (1 - ahead))

        @pl.when(s == 0)
        def _():
            value = grad(g_in[m], h_in[m], info_ref, 3 * micro + m, own, m)
            for q in range(PARTS):
                out_ref[m, :, q * part : (q + 1) * part] = value[q]

        return carry

    lax.fori_loop(0, micro, backward, 0)

    @pl.when(s > 0)
    def _():
        for m in range(micro):
            o_on(m=m, to=s).wait_recv()
            for q in range(PARTS):
                out_ref[m, :, q * part : (q + 1) * part] = o_in[m, q]

    for copy in remote:
        copy.wait_send()

    @pl.when(s < last)
    def _():
        tell(0, s).wait_send()

    @pl.when(s > 0)
    def _():
        tell(1, s).wait_send()

    def drain(u, carry):
        send_wait(send_a, u, a_send, chips - 1)
        stays = jnp.where(u < micro, s == last, s == 0)

        @pl.when(stays)
        def _():
            send_wait(send_b, u, b_send, chips - 1)

        @pl.when(jnp.logical_not(stays))
        def _():
            send_wait(send_b, u, b_send, chips)

        return carry

    lax.fori_loop(0, 2 * micro, drain, 0)
    for m in range(micro):

        @pl.when(s < last)
        def _():
            h_on(m=m, to=s).wait_send()
            o_on(m=m, to=s).wait_send()

        @pl.when(s > 0)
        def _():
            h_back(m=m, to=s).wait_send()
            g_back(m=m, to=s).wait_send()


def body(tokens, norm_gain, w_gate, w_up, w_down, route_ids, route_gates):
    sections = lax.axis_size("section")
    chips = lax.axis_size("expert") // 2
    micro, tok, width = tokens.shape
    top = route_ids.shape[-1]
    half = w_gate.shape[-1]
    hidden = 2 * half
    cap = max(2, (4 * tok * top + 3 * chips - 1) // (3 * chips))
    blk = PARTS * cap
    part = width // PARTS
    groups = 4
    per = chips // groups
    grp = per * cap
    units = 2 * micro

    flat = route_ids[0].reshape(micro, tok * top)
    onehot = (flat[:, :, None] == jnp.arange(chips, dtype=jnp.int32)).astype(jnp.int32)
    before = jnp.cumsum(onehot, axis=1) - onehot
    position = jnp.sum(before * onehot, axis=-1)
    first = (flat * blk + position).reshape(micro, tok, top).transpose(0, 2, 1)
    offset = jnp.arange(PARTS, dtype=jnp.int32) * cap
    target = (first[:, :, None, :] + offset[None, None, :, None]).reshape(micro, top * PARTS * tok)
    gates = route_gates[0].transpose(0, 2, 1)
    gates = jnp.broadcast_to(gates[:, :, None, :], (micro, top, PARTS, tok)).reshape(micro, -1)
    pad = ((0, 0), (0, part - top * PARTS * tok))
    info = jnp.concatenate(
        [
            jnp.pad(target.astype(F32), pad),
            jnp.pad(gates, pad),
            norm_gain.reshape(PARTS, part),
            jnp.zeros((16 - 2 * micro - PARTS, part), F32),
        ]
    )

    src = jnp.arange(per * blk, dtype=jnp.int32)
    dest = (src % blk // cap) * grp + src // blk * cap + src % cap
    perm_t = (dest[:, None] == src[None, :]).astype(BF16)
    perm = (src[:, None] == dest[None, :]).astype(BF16)

    dims = (sections, chips, cap, tok, width, micro, groups, half)
    vmem = pl.BlockSpec(memory_space=pltpu.VMEM)
    hbm = pl.BlockSpec(memory_space=pl.ANY)
    dma = pltpu.SemaphoreType.DMA
    result = pl.pallas_call(
        functools.partial(kernel, dims),
        out_shape=jax.ShapeDtypeStruct((micro, tok, width), BF16),
        in_specs=[vmem] * 4 + [hbm] * 3,
        out_specs=vmem,
        scratch_shapes=[
            pltpu.VMEM((width, hidden), BF16),
            pltpu.VMEM((width, hidden), BF16),
            pltpu.VMEM((hidden, width), BF16),
            pltpu.VMEM((2, 16, part), F32),
            pltpu.VMEM((3, top * PARTS * tok, 16), F32),
        ]
        + [pltpu.VMEM((micro, PARTS, tok, part), BF16)] * 6
        + [pltpu.VMEM((units, chips, blk, part), BF16)] * 3
        + [
            pltpu.VMEM((2 * units, chips, blk, part), BF16),
            pltpu.VMEM((micro, chips * blk, top * PARTS * tok), BF16),
            pltpu.VMEM((3, micro, top * PARTS * tok, chips * blk), BF16),
            pltpu.VMEM((top * PARTS * tok, part), BF16),
            pltpu.VMEM((groups, PARTS * grp, part), BF16),
            pltpu.VMEM((chips * cap, width), BF16),
            pltpu.VMEM((micro, hidden // 256, chips * cap, 256), F32),
            pltpu.VMEM((micro, hidden // 256, chips * cap, 256), F32),
            pltpu.VMEM((chips * cap, hidden), BF16),
            pltpu.VMEM((chips * cap, hidden), BF16),
            dma((3,)),
            dma((3,)),
            dma((3,)),
            dma((2,)),
            dma((2,)),
            dma((units,)),
            dma((units, groups)),
            dma((units,)),
            dma((2 * units, groups)),
            dma((4, micro)),
            dma((4, micro)),
            pltpu.SemaphoreType.REGULAR,
        ],
        compiler_params=pltpu.CompilerParams(
            collective_id=0, has_side_effects=True, vmem_limit_bytes=60 * 1024 * 1024
        ),
        name="relay",
    )(
        tokens,
        info,
        perm,
        perm_t,
        w_gate[0],
        w_up[0],
        w_down[0],
    )
    return result[None]


def solution(mesh):
    in_specs = (
        P(None, "expert", None),
        P("section", None),
        P("section", None, "expert"),
        P("section", None, "expert"),
        P("section", "expert", None),
        P("section", None, "expert", None),
        P("section", None, "expert", None),
    )
    out_specs = P("section", None, "expert", None)
    return jax.shard_map(body, mesh=mesh, in_specs=in_specs, out_specs=out_specs, check_vma=False)
```

```python
import functools

import jax
import jax.numpy as jnp
from jax import lax
from jax.experimental import pallas as pl
from jax.experimental.pallas import tpu as pltpu
from jax.sharding import PartitionSpec as P

EPS = 1e-06
PARTS = 4
CHUNKS = 4
MESH = pl.DeviceIdType.MESH
F32 = jnp.float32
BF16 = jnp.bfloat16


def mm(a, b):
    return jnp.dot(a, b, preferred_element_type=F32)


def mm_nt(a, b):
    return lax.dot_general(a, b, (((1,), (1,)), ((), ())), preferred_element_type=F32)


def kernel(
    dims,
    tokens_ref,
    info_ref,
    perm_ref,
    perm_t_ref,
    w_gate_ref,
    w_up_ref,
    w_down_ref,
    out_ref,
    wg,
    wu,
    wd,
    info_near,
    cols,
    h_in,
    h_prev,
    h_next,
    g_in,
    g_next,
    o_in,
    send_a,
    recv_a,
    send_b,
    recv_b,
    spread,
    collect,
    stage,
    pieces,
    rows,
    pre_g,
    pre_u,
    act_a,
    act_b,
    w_local,
    w_send,
    w_recv,
    i_send,
    i_recv,
    a_send,
    a_recv,
    b_send,
    b_recv,
    x_send,
    x_recv,
    turn,
):
    sections, chips, cap, tok, width, micro, groups, half = dims
    blk = PARTS * cap
    part = width // PARTS
    per = chips // groups
    grp_rows = per * cap
    run = groups // CHUNKS
    hidden = 2 * half
    n = PARTS * tok
    step = 256
    mark = 1
    last = sections - 1
    prev, own, after = 0, 1, 2
    s = lax.axis_index("section")
    ex = lax.axis_index("expert")
    core = lax.rem(ex, 2)
    chip = lax.div(ex, 2)
    mate = 2 * chip + (1 - core)
    my_group = lax.div(chip, per)

    def other(j):
        g = lax.rem(my_group + lax.div(j, per), groups)
        return g * per + lax.rem(chip + j, per)

    barrier = pltpu.get_barrier_semaphore()

    def greet(section, j):
        pl.semaphore_signal(
            barrier,
            inc=1,
            device_id={"section": section, "expert": 2 * other(j) + core},
            device_id_type=MESH,
        )

    def greet_own(j, carry):
        greet(s, j)
        return carry

    lax.fori_loop(1, chips, greet_own, 0)
    pl.semaphore_signal(barrier, inc=1, device_id={"expert": mate}, device_id_type=MESH)

    @pl.when(s > 0)
    def _():
        def one(j, carry):
            greet(s - 1, j)
            return carry

        lax.fori_loop(0, chips, one, 0)

    @pl.when(s < last)
    def _():
        def one(j, carry):
            greet(s + 1, j)
            return carry

        lax.fori_loop(0, chips, one, 0)

    local = [
        pltpu.make_async_copy(w_gate_ref, wg.at[:, :half], w_local.at[0]),
        pltpu.make_async_copy(w_up_ref, wu.at[:, :half], w_local.at[1]),
        pltpu.make_async_copy(w_down_ref, wd.at[:half, :], w_local.at[2]),
    ]
    for copy in local:
        copy.start()

    def columns(which, ref):
        cols[which] = jnp.transpose(ref[:, : 2 * n])

    def build(which, m):
        for k in range(2):
            at = k * n
            sub = cols[which, at : at + n, :][:, m : m + 1]
            ids = lax.broadcasted_iota(jnp.int32, (n, chips * blk), 1)
            collect[which, m, at : at + n, :] = jnp.where(
                ids == sub.astype(jnp.int32), 1.0, 0.0
            ).astype(BF16)

    for m in range(micro):
        for k in range(2):
            at = k * n
            lane = info_ref[m : m + 1, at : at + n].astype(jnp.int32)
            ids = lax.broadcasted_iota(jnp.int32, (chips * blk, n), 0)
            spread[m, :, at : at + n] = jnp.where(ids == lane, 1.0, 0.0).astype(BF16)

    ahead = lax.convert_element_type(s > 0, jnp.int32)
    behind = lax.convert_element_type(s < last, jnp.int32)
    pl.semaphore_wait(barrier, chips + chips * ahead + chips * behind)

    remote = [
        pltpu.make_async_remote_copy(
            src, dst, w_send.at[i], w_recv.at[i], device_id={"expert": mate}, device_id_type=MESH
        )
        for i, (src, dst) in enumerate(
            (
                (w_gate_ref, wg.at[:, half:]),
                (w_up_ref, wu.at[:, half:]),
                (w_down_ref, wd.at[half:, :]),
            )
        )
    ]
    for copy in remote:
        copy.start()

    def tell(slot, to):
        return pltpu.make_async_remote_copy(
            info_ref,
            info_near.at[slot],
            i_send.at[slot],
            i_recv.at[slot],
            device_id={"section": to},
            device_id_type=MESH,
        )

    @pl.when(s < last)
    def _():
        tell(0, s + 1).start()

    @pl.when(s > 0)
    def _():
        tell(1, s - 1).start()

    def hop(src, dst, m, kind, to):
        return pltpu.make_async_remote_copy(
            src.at[m],
            dst.at[m],
            x_send.at[kind, m],
            x_recv.at[kind, m],
            device_id={"section": to},
            device_id_type=MESH,
        )

    h_on = functools.partial(hop, h_in, h_prev, kind=0)
    h_back = functools.partial(hop, h_in, h_next, kind=1)
    g_back = functools.partial(hop, g_in, g_next, kind=2)
    o_on = functools.partial(hop, g_in, o_in, kind=3)

    def send_wait(buf, u, sem, count):
        view = buf.at[u, pl.ds(0, count)]
        pltpu.make_async_copy(view, view, sem.at[u]).wait()

    def group_wait(buf, u, i, sem):
        g = lax.rem(my_group + groups - i, groups)
        view = buf.at[u, pl.ds(g * per, per)]
        pltpu.make_async_copy(view, view, sem.at[u, g]).wait()
        return g

    def dispatch(u, m):
        send_a[u] = mm(
            spread[m] if stage_full[0] else spread[m, :, :n] + spread[m, :, n:],
            stage[...] if stage_full[0] else stage[:n, :],
        ).reshape(chips, blk, part).astype(BF16)

        @pl.when(core == 1)
        def _():
            pl.semaphore_wait(turn, 1)

        def one(j, carry):
            d = other(j)
            pltpu.make_async_remote_copy(
                send_a.at[u, d],
                recv_a.at[u, chip],
                a_send.at[u],
                a_recv.at[u, my_group],
                device_id={"expert": 2 * d + core},
                device_id_type=MESH,
            ).start()
            return carry

        lax.fori_loop(1, chips, one, 0)
        pltpu.make_async_copy(send_a.at[u, chip], recv_a.at[u, chip], a_recv.at[u, my_group]).start()

    def arrive(u, c):
        def one(t, carry):
            i = c * run + t
            g = group_wait(recv_a, u, i, a_recv)

            @pl.when((core == 0) & (i == mark))
            def _():
                pl.semaphore_signal(turn, inc=1, device_id={"expert": mate}, device_id_type=MESH)

            got = recv_a[u, pl.ds(g * per, per)].astype(F32).reshape(per * blk, part).astype(BF16)
            sorted_rows = mm(perm_ref[...], got).astype(BF16)
            for q in range(PARTS):
                rows[pl.ds(t * grp_rows, grp_rows), q * part : (q + 1) * part] = sorted_rows[
                    q * grp_rows : (q + 1) * grp_rows
                ]
            return carry

        lax.fori_loop(0, run, one, 0)

    def give_back(u, c, to, slot):
        def one(t, carry):
            g = lax.rem(my_group + groups - c * run - t, groups)
            got = mm(perm_t_ref[...], pieces[t])
            send_b[u, pl.ds(g * per, per)] = got.reshape(per, blk, part).astype(BF16)

            def block(j, inner):
                d = g * per + lax.rem(chip + j, per)

                @pl.when(jnp.logical_or(d != chip, to != s))
                def _():
                    pltpu.make_async_remote_copy(
                        send_b.at[u, d],
                        recv_b.at[slot, chip],
                        b_send.at[u],
                        b_recv.at[slot, my_group],
                        device_id={"section": to, "expert": 2 * d + core},
                        device_id_type=MESH,
                    ).start()

                return inner

            return lax.fori_loop(0, per, block, carry)

        lax.fori_loop(0, run, one, 0)

        @pl.when((to == s) & (c == 0))
        def _():
            pltpu.make_async_copy(
                send_b.at[u, chip], recv_b.at[slot, chip], b_recv.at[slot, my_group]
            ).start()

    def wait_back(slot):
        def one(i, carry):
            group_wait(recv_b, slot, i, b_recv)
            return carry

        lax.fori_loop(0, groups, one, 0)
        return recv_b[slot].astype(F32).reshape(chips * blk, part).astype(BF16)

    def put_pieces(q, value):
        for t in range(run):
            pieces[t, pl.ds(q * grp_rows, grp_rows), :] = value[t * grp_rows : (t + 1) * grp_rows]

    def gate_column(which, m):
        return jnp.where(m == 0, cols[which][:, micro : micro + 1], cols[which][:, micro + 1 : micro + 2])

    def inverse_rms(h):
        total = jnp.sum(jnp.sum(h * h, axis=-1, keepdims=True), axis=0)
        return lax.rsqrt(total / width + EPS)

    def mix(h, slot, which, m):
        picked = mm(collect[which, m], wait_back(slot)) * gate_column(which, m)
        mixture = picked[:n] + picked[n:]
        return (h.astype(F32) + mixture.reshape(PARTS, tok, part)).astype(BF16)

    def grad(g, h, gain, slot, which, m):
        sel = collect[which, m, :n] + collect[which, m, n:]
        total = mm(sel, wait_back(slot)).reshape(PARTS, tok, part)
        h = h.astype(F32)
        inv = inverse_rms(h)
        weighted = total * jnp.stack([gain[2 * micro + q : 2 * micro + q + 1, :] for q in range(PARTS)])
        dot = jnp.sum(jnp.sum(h * weighted, axis=-1, keepdims=True), axis=0) / width
        change = inv[None] * weighted - h * (inv * inv * inv * dot)[None]
        return (g.astype(F32) + change).astype(BF16)

    columns(own, info_ref)
    stage_full = [False]

    @pl.when(s > 0)
    def _():
        tell(0, s).wait_recv()
        columns(prev, info_near.at[0])
        for m in range(micro):
            build(prev, m)

    def forward(m, carry):
        u = m

        @pl.when(s == 0)
        def _():
            for q in range(PARTS):
                h_in[m, q] = tokens_ref[m, :, q * part : (q + 1) * part]

        @pl.when(s > 0)
        def _():
            h_on(m=m, to=s).wait_recv()
            h_in[m] = mix(h_prev[m], m, prev, m)

        inv = inverse_rms(h_in[m].astype(F32))
        for q in range(PARTS):
            gain = info_ref[2 * micro + q : 2 * micro + q + 1, :]
            stage[pl.ds(q * tok, tok), :] = (h_in[m, q].astype(F32) * inv * gain).astype(BF16)
        dispatch(u, m)

        @pl.when(s < last)
        def _():
            h_on(m=m, to=s + 1).start()

        @pl.when(s > 0)
        def _():
            h_back(m=m, to=s - 1).start()

        @pl.when(m == 0)
        def _():
            for copy in local:
                copy.wait()
            for copy in remote:
                copy.wait_recv()
            for i in range(micro):
                build(own, i)

            @pl.when(s < last)
            def _():
                tell(1, s).wait_recv()
                columns(after, info_near.at[1])
                for i in range(micro):
                    build(after, i)

        def chunk(c, carry):
            arrive(u, c)

            def first(i, carry):
                at = pl.ds(pl.multiple_of(i * step, step), step)
                gate = mm(rows[...], wg[:, at])
                up = mm(rows[...], wu[:, at])
                pre_g[m, c, i] = gate
                pre_u[m, c, i] = up
                act_a[:, at] = (gate * jax.nn.sigmoid(gate) * up).astype(BF16)
                return carry

            lax.fori_loop(0, hidden // step, first, 0)

            def second(q, carry):
                at = pl.ds(pl.multiple_of(q * part, part), part)
                put_pieces(q, mm(act_a[...], wd[:, at]).astype(BF16))
                return carry

            lax.fori_loop(0, PARTS, second, 0)
            give_back(u, c, jnp.minimum(s + 1, last), m + micro * (1 - behind))
            return carry

        lax.fori_loop(0, CHUNKS, chunk, 0)

        @pl.when(s == last)
        def _():
            g_in[m] = mix(h_in[m], micro + m, own, m)

        return carry

    lax.fori_loop(0, micro, forward, 0)
    stage_full[0] = True

    def backward(m, carry):
        u = micro + m

        @pl.when(s < last)
        def _():
            g_back(m=m, to=s).wait_recv()
            h_back(m=m, to=s).wait_recv()
            g_in[m] = grad(g_next[m], h_next[m], info_near.at[1], 2 * micro + m, after, m)

        upstream = g_in[m].astype(F32).reshape(n, part)
        gates = gate_column(own, m)
        stage[:n, :] = (gates[:n] * upstream).astype(BF16)
        stage[n:, :] = (gates[n:] * upstream).astype(BF16)
        dispatch(u, m)

        @pl.when(s > 0)
        def _():
            g_back(m=m, to=s - 1).start()

        @pl.when(s < last)
        def _():
            o_on(m=m, to=s + 1).start()

        def chunk(c, carry):
            arrive(u, c)

            def first(i, carry):
                at = pl.ds(pl.multiple_of(i * step, step), step)
                grad_hidden = mm_nt(rows[...], wd[at, :])
                gate = pre_g[m, c, i]
                up = pre_u[m, c, i]
                logistic = jax.nn.sigmoid(gate)
                slope = logistic * (1.0 + gate * (1.0 - logistic))
                act_a[:, at] = (grad_hidden * up * slope).astype(BF16)
                act_b[:, at] = (grad_hidden * gate * logistic).astype(BF16)
                return carry

            lax.fori_loop(0, hidden // step, first, 0)

            def second(q, carry):
                at = pl.ds(pl.multiple_of(q * part, part), part)
                value = mm_nt(act_a[...], wg[at, :]) + mm_nt(act_b[...], wu[at, :])
                put_pieces(q, value.astype(BF16))
                return carry

            lax.fori_loop(0, PARTS, second, 0)
            give_back(u, c, jnp.maximum(s - 1, 0), 2 * micro + m + micro * (1 - ahead))
            return carry

        lax.fori_loop(0, CHUNKS, chunk, 0)

        @pl.when(s == 0)
        def _():
            value = grad(g_in[m], h_in[m], info_ref, 3 * micro + m, own, m)
            for q in range(PARTS):
                out_ref[m, :, q * part : (q + 1) * part] = value[q]

        return carry

    lax.fori_loop(0, micro, backward, 0)

    @pl.when(s > 0)
    def _():
        for m in range(micro):
            o_on(m=m, to=s).wait_recv()
            for q in range(PARTS):
                out_ref[m, :, q * part : (q + 1) * part] = o_in[m, q]

    for copy in remote:
        copy.wait_send()

    @pl.when(s < last)
    def _():
        tell(0, s).wait_send()

    @pl.when(s > 0)
    def _():
        tell(1, s).wait_send()

    def drain(u, carry):
        send_wait(send_a, u, a_send, chips - 1)
        stays = jnp.where(u < micro, s == last, s == 0)

        @pl.when(stays)
        def _():
            send_wait(send_b, u, b_send, chips - 1)

        @pl.when(jnp.logical_not(stays))
        def _():
            send_wait(send_b, u, b_send, chips)

        return carry

    lax.fori_loop(0, 2 * micro, drain, 0)
    for m in range(micro):

        @pl.when(s < last)
        def _():
            h_on(m=m, to=s).wait_send()
            o_on(m=m, to=s).wait_send()

        @pl.when(s > 0)
        def _():
            h_back(m=m, to=s).wait_send()
            g_back(m=m, to=s).wait_send()


def body(tokens, norm_gain, w_gate, w_up, w_down, route_ids, route_gates):
    sections = lax.axis_size("section")
    chips = lax.axis_size("expert") // 2
    micro, tok, width = tokens.shape
    top = route_ids.shape[-1]
    half = w_gate.shape[-1]
    hidden = 2 * half
    cap = max(2, (4 * tok * top + 3 * chips - 1) // (3 * chips))
    blk = PARTS * cap
    part = width // PARTS
    groups = 4
    per = chips // groups
    grp = per * cap
    units = 2 * micro
    chunk_rows = chips * cap // CHUNKS

    flat = route_ids[0].reshape(micro, tok * top)
    onehot = (flat[:, :, None] == jnp.arange(chips, dtype=jnp.int32)).astype(jnp.int32)
    before = jnp.cumsum(onehot, axis=1) - onehot
    position = jnp.sum(before * onehot, axis=-1)
    first = (flat * blk + position).reshape(micro, tok, top).transpose(0, 2, 1)
    offset = jnp.arange(PARTS, dtype=jnp.int32) * cap
    target = (first[:, :, None, :] + offset[None, None, :, None]).reshape(micro, top * PARTS * tok)
    gates = route_gates[0].transpose(0, 2, 1)
    gates = jnp.broadcast_to(gates[:, :, None, :], (micro, top, PARTS, tok)).reshape(micro, -1)
    pad = ((0, 0), (0, part - top * PARTS * tok))
    info = jnp.concatenate(
        [
            jnp.pad(target.astype(F32), pad),
            jnp.pad(gates, pad),
            norm_gain.reshape(PARTS, part),
            jnp.zeros((16 - 2 * micro - PARTS, part), F32),
        ]
    )

    src = jnp.arange(per * blk, dtype=jnp.int32)
    dest = (src % blk // cap) * grp + src // blk * cap + src % cap
    perm_t = (dest[:, None] == src[None, :]).astype(BF16)
    perm = (src[:, None] == dest[None, :]).astype(BF16)

    dims = (sections, chips, cap, tok, width, micro, groups, half)
    vmem = pl.BlockSpec(memory_space=pltpu.VMEM)
    hbm = pl.BlockSpec(memory_space=pl.ANY)
    dma = pltpu.SemaphoreType.DMA
    result = pl.pallas_call(
        functools.partial(kernel, dims),
        out_shape=jax.ShapeDtypeStruct((micro, tok, width), BF16),
        in_specs=[vmem] * 4 + [hbm] * 3,
        out_specs=vmem,
        scratch_shapes=[
            pltpu.VMEM((width, hidden), BF16),
            pltpu.VMEM((width, hidden), BF16),
            pltpu.VMEM((hidden, width), BF16),
            pltpu.VMEM((2, 16, part), F32),
            pltpu.VMEM((3, top * PARTS * tok, 16), F32),
        ]
        + [pltpu.VMEM((micro, PARTS, tok, part), BF16)] * 6
        + [pltpu.VMEM((units, chips, blk, part), BF16)] * 3
        + [
            pltpu.VMEM((2 * units, chips, blk, part), BF16),
            pltpu.VMEM((micro, chips * blk, top * PARTS * tok), BF16),
            pltpu.VMEM((3, micro, top * PARTS * tok, chips * blk), BF16),
            pltpu.VMEM((top * PARTS * tok, part), BF16),
            pltpu.VMEM((groups // CHUNKS, PARTS * grp, part), BF16),
            pltpu.VMEM((chunk_rows, width), BF16),
            pltpu.VMEM((micro, CHUNKS, hidden // 256, chunk_rows, 256), F32),
            pltpu.VMEM((micro, CHUNKS, hidden // 256, chunk_rows, 256), F32),
            pltpu.VMEM((chunk_rows, hidden), BF16),
            pltpu.VMEM((chunk_rows, hidden), BF16),
            dma((3,)),
            dma((3,)),
            dma((3,)),
            dma((2,)),
            dma((2,)),
            dma((units,)),
            dma((units, groups)),
            dma((units,)),
            dma((2 * units, groups)),
            dma((4, micro)),
            dma((4, micro)),
            pltpu.SemaphoreType.REGULAR,
        ],
        compiler_params=pltpu.CompilerParams(
            collective_id=0, has_side_effects=True, vmem_limit_bytes=60 * 1024 * 1024
        ),
        name="relay",
    )(
        tokens,
        info,
        perm,
        perm_t,
        w_gate[0],
        w_up[0],
        w_down[0],
    )
    return result[None]


def solution(mesh):
    in_specs = (
        P(None, "expert", None),
        P("section", None),
        P("section", None, "expert"),
        P("section", None, "expert"),
        P("section", "expert", None),
        P("section", None, "expert", None),
        P("section", None, "expert", None),
    )
    out_specs = P("section", None, "expert", None)
    return jax.shard_map(body, mesh=mesh, in_specs=in_specs, out_specs=out_specs, check_vma=False)
```

```python
import functools

import jax
import jax.numpy as jnp
from jax import lax
from jax.experimental import pallas as pl
from jax.experimental.pallas import tpu as pltpu
from jax.sharding import PartitionSpec as P

EPS = 1e-06
PARTS = 4
CHUNKS = 4
MESH = pl.DeviceIdType.MESH
F32 = jnp.float32
BF16 = jnp.bfloat16


def mm(a, b):
    return jnp.dot(a, b, preferred_element_type=F32)


def mm_nt(a, b):
    return lax.dot_general(a, b, (((1,), (1,)), ((), ())), preferred_element_type=F32)


def kernel(
    dims,
    tokens_ref,
    info_ref,
    perm_ref,
    perm_t_ref,
    w_gate_ref,
    w_up_ref,
    w_down_ref,
    out_ref,
    wg,
    wu,
    wd,
    info_near,
    cols,
    h_in,
    h_prev,
    h_next,
    g_in,
    g_next,
    o_in,
    send_a,
    recv_a,
    send_b,
    recv_b,
    spread,
    collect,
    stage,
    pieces,
    rows,
    pre_g,
    pre_u,
    act_a,
    act_b,
    w_local,
    w_send,
    w_recv,
    i_send,
    i_recv,
    a_send,
    a_recv,
    b_send,
    b_recv,
    x_send,
    x_recv,
    turn,
    entered,
):
    sections, chips, cap, tok, width, micro, groups, half = dims
    blk = PARTS * cap
    part = width // PARTS
    per = chips // groups
    grp_rows = per * cap
    run = groups // CHUNKS
    hidden = 2 * half
    n = PARTS * tok
    step = 256
    mark = 1
    last = sections - 1
    prev, own, after = 0, 1, 2
    s = lax.axis_index("section")
    ex = lax.axis_index("expert")
    core = lax.rem(ex, 2)
    chip = lax.div(ex, 2)
    mate = 2 * chip + (1 - core)
    my_group = lax.div(chip, per)

    def other(j):
        g = lax.rem(my_group + lax.div(j, per), groups)
        return g * per + lax.rem(chip + j, per)

    barrier = pltpu.get_barrier_semaphore()

    def greet(j, carry):
        pl.semaphore_signal(
            barrier, inc=1, device_id={"expert": 2 * other(j) + core}, device_id_type=MESH
        )
        return carry

    turns = jnp.where(s == last, micro, 2 * micro)

    lax.fori_loop(1, chips, greet, 0)
    pl.semaphore_signal(barrier, inc=1, device_id={"expert": mate}, device_id_type=MESH)

    @pl.when(s > 0)
    def _():
        pl.semaphore_signal(barrier, inc=1, device_id={"section": s - 1}, device_id_type=MESH)

    @pl.when(s < last)
    def _():
        pl.semaphore_signal(barrier, inc=1, device_id={"section": s + 1}, device_id_type=MESH)

    local = [
        pltpu.make_async_copy(w_gate_ref, wg.at[:, :half], w_local.at[0]),
        pltpu.make_async_copy(w_up_ref, wu.at[:, :half], w_local.at[1]),
        pltpu.make_async_copy(w_down_ref, wd.at[:half, :], w_local.at[2]),
    ]
    for copy in local:
        copy.start()

    def columns(which, ref):
        cols[which] = jnp.transpose(ref[:, : 2 * n])

    def build(which, m):
        for k in range(2):
            at = k * n
            sub = cols[which, at : at + n, :][:, m : m + 1]
            ids = lax.broadcasted_iota(jnp.int32, (n, chips * blk), 1)
            collect[which, m, at : at + n, :] = jnp.where(
                ids == sub.astype(jnp.int32), 1.0, 0.0
            ).astype(BF16)

    def build_spread(m, ref=info_ref, place=0):
        for k in range(2):
            at = k * n
            lane = ref[m : m + 1, at : at + n].astype(jnp.int32)
            ids = lax.broadcasted_iota(jnp.int32, (chips * blk, n), 0)
            spread[place + m, :, at : at + n] = jnp.where(ids == lane, 1.0, 0.0).astype(BF16)

    build_spread(0)
    ahead = lax.convert_element_type(s > 0, jnp.int32)
    behind = lax.convert_element_type(s < last, jnp.int32)
    pl.semaphore_wait(barrier, chips + ahead + behind)

    @pl.when(s > 0)
    def _():
        pl.semaphore_signal(entered.at[1], inc=1, device_id={"section": s - 1}, device_id_type=MESH)

    @pl.when(s < last)
    def _():
        pl.semaphore_signal(entered.at[0], inc=1, device_id={"section": s + 1}, device_id_type=MESH)

    remote = [
        pltpu.make_async_remote_copy(
            src, dst, w_send.at[i], w_recv.at[i], device_id={"expert": mate}, device_id_type=MESH
        )
        for i, (src, dst) in enumerate(
            (
                (w_gate_ref, wg.at[:, half:]),
                (w_up_ref, wu.at[:, half:]),
                (w_down_ref, wd.at[half:, :]),
            )
        )
    ]
    for copy in remote:
        copy.start()

    def tell(slot, to):
        return pltpu.make_async_remote_copy(
            info_ref,
            info_near.at[slot],
            i_send.at[slot],
            i_recv.at[slot],
            device_id={"section": to},
            device_id_type=MESH,
        )

    @pl.when(s < last)
    def _():
        tell(0, s + 1).start()

    @pl.when(s > 0)
    def _():
        tell(1, s - 1).start()

    def hop(src, dst, m, kind, to):
        return pltpu.make_async_remote_copy(
            src.at[m],
            dst.at[m],
            x_send.at[kind, m],
            x_recv.at[kind, m],
            device_id={"section": to},
            device_id_type=MESH,
        )

    h_on = functools.partial(hop, h_in, h_prev, kind=0)
    h_back = functools.partial(hop, h_in, h_next, kind=1)
    g_back = functools.partial(hop, g_in, g_next, kind=2)
    o_on = functools.partial(hop, g_in, o_in, kind=3)

    def send_wait(buf, u, sem, count):
        view = buf.at[u, pl.ds(0, count)]
        pltpu.make_async_copy(view, view, sem.at[u]).wait()

    def group_wait(buf, u, i, sem):
        g = lax.rem(my_group + groups - i, groups)
        view = buf.at[u, pl.ds(g * per, per)]
        pltpu.make_async_copy(view, view, sem.at[u, g]).wait()
        return g

    def fill(u, sel, value):
        send_a[u] = mm(sel, value).reshape(chips, blk, part).astype(BF16)

    def dispatch(u):
        @pl.when(jnp.logical_or(core == 1, u > 0))
        def _():
            pl.semaphore_wait(turn, 1)

        def one(j, carry):
            d = other(j)
            pltpu.make_async_remote_copy(
                send_a.at[u, d],
                recv_a.at[u, chip],
                a_send.at[u],
                a_recv.at[u, my_group],
                device_id={"expert": 2 * d + core},
                device_id_type=MESH,
            ).start()
            return carry

        lax.fori_loop(1, chips, one, 0)
        pltpu.make_async_copy(send_a.at[u, chip], recv_a.at[u, chip], a_recv.at[u, my_group]).start()

    def dispatch_last(m):
        def one(j, carry):
            d = other(j)
            pltpu.make_async_remote_copy(
                send_a.at[2 * micro + m, d],
                recv_a.at[micro + m, chip],
                a_send.at[2 * micro + m],
                a_recv.at[micro + m, my_group],
                device_id={"section": last, "expert": 2 * d + core},
                device_id_type=MESH,
            ).start()
            return carry

        lax.fori_loop(0, chips, one, 0)

    def arrive(u, c):
        def one(t, carry):
            i = c * run + t
            g = group_wait(recv_a, u, i, a_recv)

            got = recv_a[u, pl.ds(g * per, per)].astype(F32).reshape(per * blk, part).astype(BF16)
            sorted_rows = mm(perm_ref[...], got).astype(BF16)
            for q in range(PARTS):
                rows[pl.ds(t * grp_rows, grp_rows), q * part : (q + 1) * part] = sorted_rows[
                    q * grp_rows : (q + 1) * grp_rows
                ]
            return carry

        lax.fori_loop(0, run, one, 0)

    def give_back(u, c, to, slot):
        def one(t, carry):
            g = lax.rem(my_group + groups - c * run - t, groups)
            got = mm(perm_t_ref[...], pieces[t])
            send_b[u, pl.ds(g * per, per)] = got.reshape(per, blk, part).astype(BF16)

            def block(j, inner):
                d = g * per + lax.rem(chip + j, per)

                @pl.when(jnp.logical_or(d != chip, to != s))
                def _():
                    pltpu.make_async_remote_copy(
                        send_b.at[u, d],
                        recv_b.at[slot, chip],
                        b_send.at[u],
                        b_recv.at[slot, my_group],
                        device_id={"section": to, "expert": 2 * d + core},
                        device_id_type=MESH,
                    ).start()

                return inner

            return lax.fori_loop(0, per, block, carry)

        lax.fori_loop(0, run, one, 0)

        @pl.when((u < turns - 1 + (1 - core)) & (c == mark))
        def _():
            pl.semaphore_signal(turn, inc=1, device_id={"expert": mate}, device_id_type=MESH)

        @pl.when((to == s) & (c == 0))
        def _():
            pltpu.make_async_copy(
                send_b.at[u, chip], recv_b.at[slot, chip], b_recv.at[slot, my_group]
            ).start()

    def wait_back(slot):
        def one(i, carry):
            group_wait(recv_b, slot, i, b_recv)
            return carry

        lax.fori_loop(0, groups, one, 0)
        return recv_b[slot].astype(F32).reshape(chips * blk, part).astype(BF16)

    def put_pieces(q, value):
        for t in range(run):
            pieces[t, pl.ds(q * grp_rows, grp_rows), :] = value[t * grp_rows : (t + 1) * grp_rows]

    def gate_column(which, m):
        return jnp.where(m == 0, cols[which][:, micro : micro + 1], cols[which][:, micro + 1 : micro + 2])

    def inverse_rms(h):
        total = jnp.sum(jnp.sum(h * h, axis=-1, keepdims=True), axis=0)
        return lax.rsqrt(total / width + EPS)

    def mix(h, slot, which, m):
        picked = mm(collect[which, m], wait_back(slot)) * gate_column(which, m)
        mixture = picked[:n] + picked[n:]
        return (h.astype(F32) + mixture.reshape(PARTS, tok, part)).astype(BF16)

    def grad(g, h, gain, slot, which, m):
        sel = collect[which, m, :n] + collect[which, m, n:]
        total = mm(sel, wait_back(slot)).reshape(PARTS, tok, part)
        h = h.astype(F32)
        inv = inverse_rms(h)
        weighted = total * jnp.stack([gain[2 * micro + q : 2 * micro + q + 1, :] for q in range(PARTS)])
        dot = jnp.sum(jnp.sum(h * weighted, axis=-1, keepdims=True), axis=0) / width
        change = inv[None] * weighted - h * (inv * inv * inv * dot)[None]
        return (g.astype(F32) + change).astype(BF16)


    def later_tables():
        columns(own, info_ref)
        for m in range(micro):
            build(own, m)

        @pl.when(s < last)
        def _():
            tell(1, s).wait_recv()
            columns(after, info_near.at[1])
            for m in range(micro):
                build(after, m)

            @pl.when(s == last - 1)
            def _():
                for m in range(micro):
                    build_spread(m, info_near.at[1], micro)

    @pl.when(s > 0)
    def _():
        build_spread(1)
        pl.semaphore_wait(entered.at[0], 1)
        tell(0, s).wait_recv()
        columns(prev, info_near.at[0])
        for m in range(micro):
            build(prev, m)
        later_tables()

    def forward(m, carry):
        u = m

        @pl.when(s == 0)
        def _():
            for q in range(PARTS):
                h_in[m, q] = tokens_ref[m, :, q * part : (q + 1) * part]

        @pl.when(s > 0)
        def _():
            h_on(m=m, to=s).wait_recv()
            h_in[m] = mix(h_prev[m], m, prev, m)

        inv = inverse_rms(h_in[m].astype(F32))
        for q in range(PARTS):
            gain = info_ref[2 * micro + q : 2 * micro + q + 1, :]
            stage[pl.ds(q * tok, tok), :] = (h_in[m, q].astype(F32) * inv * gain).astype(BF16)
        fill(u, spread[m, :, :n] + spread[m, :, n:], stage[:n, :])
        dispatch(u)

        @pl.when(s < last)
        def _():
            h_on(m=m, to=s + 1).start()

        @pl.when(s > 0)
        def _():
            h_back(m=m, to=s - 1).start()

        @pl.when(m == 0)
        def _():
            for copy in local:
                copy.wait()
            for copy in remote:
                copy.wait_recv()

            @pl.when(s == 0)
            def _():
                build_spread(1)

            @pl.when(s < last)
            def _():
                pl.semaphore_wait(entered.at[1], 1)

        def chunk(c, carry):
            arrive(u, c)

            def first(i, carry):
                at = pl.ds(pl.multiple_of(i * step, step), step)
                gate = mm(rows[...], wg[:, at])
                up = mm(rows[...], wu[:, at])
                pre_g[m, c, i] = gate
                pre_u[m, c, i] = up
                act_a[:, at] = (gate * jax.nn.sigmoid(gate) * up).astype(BF16)
                return carry

            lax.fori_loop(0, hidden // step, first, 0)

            def second(q, carry):
                at = pl.ds(pl.multiple_of(q * part, part), part)
                put_pieces(q, mm(act_a[...], wd[:, at]).astype(BF16))
                return carry

            lax.fori_loop(0, PARTS, second, 0)
            give_back(u, c, jnp.where(s == last, last - 1, s + 1), m + micro * (1 - behind))
            return carry

        lax.fori_loop(0, CHUNKS, chunk, 0)

        return carry

    lax.fori_loop(0, micro, forward, 0)

    def scale(value, which, m):
        upstream = value.astype(F32).reshape(n, part)
        gates = gate_column(which, m)
        stage[:n, :] = (gates[:n] * upstream).astype(BF16)
        stage[n:, :] = (gates[n:] * upstream).astype(BF16)

    @pl.when(s == last - 1)
    def _():
        def one(m, carry):
            h_back(m=m, to=s).wait_recv()
            g_next[m] = mix(h_next[m], micro + m, after, m)
            scale(g_next[m], after, m)
            fill(2 * micro + m, spread[micro + m], stage[...])
            dispatch_last(m)
            return carry

        lax.fori_loop(0, micro, one, 0)

    @pl.when(s == 0)
    def _():
        later_tables()

    def backward(m, carry):
        u = micro + m

        @pl.when(s < last - 1)
        def _():
            g_back(m=m, to=s).wait_recv()
            h_back(m=m, to=s).wait_recv()

        @pl.when(s < last)
        def _():
            g_in[m] = grad(g_next[m], h_next[m], info_near.at[1], 2 * micro + m, after, m)
            scale(g_in[m], own, m)
            fill(u, spread[m], stage[...])
            dispatch(u)

        @pl.when((s > 0) & (s < last))
        def _():
            g_back(m=m, to=s - 1).start()

        @pl.when(s < last)
        def _():
            o_on(m=m, to=s + 1).start()

        def chunk(c, carry):
            arrive(u, c)

            def first(i, carry):
                at = pl.ds(pl.multiple_of(i * step, step), step)
                grad_hidden = mm_nt(rows[...], wd[at, :])
                gate = pre_g[m, c, i]
                up = pre_u[m, c, i]
                logistic = jax.nn.sigmoid(gate)
                slope = logistic * (1.0 + gate * (1.0 - logistic))
                act_a[:, at] = (grad_hidden * up * slope).astype(BF16)
                act_b[:, at] = (grad_hidden * gate * logistic).astype(BF16)
                return carry

            lax.fori_loop(0, hidden // step, first, 0)

            def second(q, carry):
                at = pl.ds(pl.multiple_of(q * part, part), part)
                value = mm_nt(act_a[...], wg[at, :]) + mm_nt(act_b[...], wu[at, :])
                put_pieces(q, value.astype(BF16))
                return carry

            lax.fori_loop(0, PARTS, second, 0)
            give_back(u, c, jnp.maximum(s - 1, 0), 2 * micro + m + micro * (1 - ahead))
            return carry

        lax.fori_loop(0, CHUNKS, chunk, 0)

        @pl.when(s == 0)
        def _():
            value = grad(g_in[m], h_in[m], info_ref, 3 * micro + m, own, m)
            for q in range(PARTS):
                out_ref[m, :, q * part : (q + 1) * part] = value[q]

        return carry

    lax.fori_loop(0, micro, backward, 0)

    @pl.when(s > 0)
    def _():
        for m in range(micro):
            o_on(m=m, to=s).wait_recv()
            for q in range(PARTS):
                out_ref[m, :, q * part : (q + 1) * part] = o_in[m, q]

    for copy in remote:
        copy.wait_send()

    @pl.when(s < last)
    def _():
        tell(0, s).wait_send()

    @pl.when(s > 0)
    def _():
        tell(1, s).wait_send()

    def drain(u, carry):
        @pl.when(u < turns)
        def _():
            send_wait(send_a, u, a_send, chips - 1)

        stays = (u >= micro) & (s == 0)

        @pl.when(stays)
        def _():
            send_wait(send_b, u, b_send, chips - 1)

        @pl.when(jnp.logical_not(stays))
        def _():
            send_wait(send_b, u, b_send, chips)

        return carry

    lax.fori_loop(0, 2 * micro, drain, 0)
    for m in range(micro):

        @pl.when(s < last)
        def _():
            h_on(m=m, to=s).wait_send()
            o_on(m=m, to=s).wait_send()

        @pl.when(s > 0)
        def _():
            h_back(m=m, to=s).wait_send()

        @pl.when((s > 0) & (s < last))
        def _():
            g_back(m=m, to=s).wait_send()

        @pl.when(s == last - 1)
        def _():
            send_wait(send_a, 2 * micro + m, a_send, chips)


def body(tokens, norm_gain, w_gate, w_up, w_down, route_ids, route_gates):
    sections = lax.axis_size("section")
    chips = lax.axis_size("expert") // 2
    micro, tok, width = tokens.shape
    top = route_ids.shape[-1]
    half = w_gate.shape[-1]
    hidden = 2 * half
    cap = max(2, (4 * tok * top + 3 * chips - 1) // (3 * chips))
    blk = PARTS * cap
    part = width // PARTS
    groups = 4
    per = chips // groups
    grp = per * cap
    units = 2 * micro
    chunk_rows = chips * cap // CHUNKS

    flat = route_ids[0].reshape(micro, tok * top)
    onehot = (flat[:, :, None] == jnp.arange(chips, dtype=jnp.int32)).astype(jnp.int32)
    before = jnp.cumsum(onehot, axis=1) - onehot
    position = jnp.sum(before * onehot, axis=-1)
    first = (flat * blk + position).reshape(micro, tok, top).transpose(0, 2, 1)
    offset = jnp.arange(PARTS, dtype=jnp.int32) * cap
    target = (first[:, :, None, :] + offset[None, None, :, None]).reshape(micro, top * PARTS * tok)
    gates = route_gates[0].transpose(0, 2, 1)
    gates = jnp.broadcast_to(gates[:, :, None, :], (micro, top, PARTS, tok)).reshape(micro, -1)
    pad = ((0, 0), (0, part - top * PARTS * tok))
    info = jnp.concatenate(
        [
            jnp.pad(target.astype(F32), pad),
            jnp.pad(gates, pad),
            norm_gain.reshape(PARTS, part),
            jnp.zeros((16 - 2 * micro - PARTS, part), F32),
        ]
    )

    src = jnp.arange(per * blk, dtype=jnp.int32)
    dest = (src % blk // cap) * grp + src // blk * cap + src % cap
    perm_t = (dest[:, None] == src[None, :]).astype(BF16)
    perm = (src[:, None] == dest[None, :]).astype(BF16)

    dims = (sections, chips, cap, tok, width, micro, groups, half)
    vmem = pl.BlockSpec(memory_space=pltpu.VMEM)
    hbm = pl.BlockSpec(memory_space=pl.ANY)
    dma = pltpu.SemaphoreType.DMA
    result = pl.pallas_call(
        functools.partial(kernel, dims),
        out_shape=jax.ShapeDtypeStruct((micro, tok, width), BF16),
        in_specs=[vmem] * 4 + [hbm] * 3,
        out_specs=vmem,
        scratch_shapes=[
            pltpu.VMEM((width, hidden), BF16),
            pltpu.VMEM((width, hidden), BF16),
            pltpu.VMEM((hidden, width), BF16),
            pltpu.VMEM((2, 16, part), F32),
            pltpu.VMEM((3, top * PARTS * tok, 16), F32),
        ]
        + [pltpu.VMEM((micro, PARTS, tok, part), BF16)] * 6
        + [
            pltpu.VMEM((units + micro, chips, blk, part), BF16),
            pltpu.VMEM((units, chips, blk, part), BF16),
            pltpu.VMEM((units, chips, blk, part), BF16),
            pltpu.VMEM((2 * units, chips, blk, part), BF16),
            pltpu.VMEM((2 * micro, chips * blk, top * PARTS * tok), BF16),
            pltpu.VMEM((3, micro, top * PARTS * tok, chips * blk), BF16),
            pltpu.VMEM((top * PARTS * tok, part), BF16),
            pltpu.VMEM((groups // CHUNKS, PARTS * grp, part), BF16),
            pltpu.VMEM((chunk_rows, width), BF16),
            pltpu.VMEM((micro, CHUNKS, hidden // 256, chunk_rows, 256), F32),
            pltpu.VMEM((micro, CHUNKS, hidden // 256, chunk_rows, 256), F32),
            pltpu.VMEM((chunk_rows, hidden), BF16),
            pltpu.VMEM((chunk_rows, hidden), BF16),
            dma((3,)),
            dma((3,)),
            dma((3,)),
            dma((2,)),
            dma((2,)),
            dma((units + micro,)),
            dma((units, groups)),
            dma((units,)),
            dma((2 * units, groups)),
            dma((4, micro)),
            dma((4, micro)),
            pltpu.SemaphoreType.REGULAR,
            pltpu.SemaphoreType.REGULAR((2,)),
        ],
        compiler_params=pltpu.CompilerParams(
            collective_id=0, has_side_effects=True, vmem_limit_bytes=60 * 1024 * 1024
        ),
        name="relay",
    )(
        tokens,
        info,
        perm,
        perm_t,
        w_gate[0],
        w_up[0],
        w_down[0],
    )
    return result[None]


def solution(mesh):
    in_specs = (
        P(None, "expert", None),
        P("section", None),
        P("section", None, "expert"),
        P("section", None, "expert"),
        P("section", "expert", None),
        P("section", None, "expert", None),
        P("section", None, "expert", None),
    )
    out_specs = P("section", None, "expert", None)
    return jax.shard_map(body, mesh=mesh, in_specs=in_specs, out_specs=out_specs, check_vma=False)
```

```python
import functools

import jax
import jax.numpy as jnp
import numpy as np
from jax import lax
from jax.experimental import pallas as pl
from jax.experimental.pallas import tpu as pltpu
from jax.sharding import PartitionSpec as P

EPS = 1e-06
PARTS = 4
CHUNKS = 4
MESH = pl.DeviceIdType.MESH
F32 = jnp.float32
BF16 = jnp.bfloat16


def mm(a, b):
    return jnp.dot(a, b, preferred_element_type=F32)


def mm_nt(a, b):
    return lax.dot_general(a, b, (((1,), (1,)), ((), ())), preferred_element_type=F32)


def kernel(
    dims,
    tokens_ref,
    info_ref,
    perm_ref,
    perm_t_ref,
    w_gate_ref,
    w_up_ref,
    w_down_ref,
    out_ref,
    wg,
    wu,
    wd,
    info_near,
    cols,
    h_in,
    h_prev,
    h_next,
    g_in,
    g_next,
    o_in,
    send_a,
    recv_a,
    send_b,
    recv_b,
    spread,
    collect,
    stage,
    pieces,
    rows,
    pre_g,
    pre_u,
    act_a,
    act_b,
    w_local,
    w_send,
    w_recv,
    i_send,
    i_recv,
    a_send,
    a_recv,
    b_send,
    b_recv,
    x_send,
    x_recv,
    turn,
    entered,
):
    sections, chips, cap, tok, width, micro, groups, half = dims
    blk = PARTS * cap
    part = width // PARTS
    per = chips // groups
    grp_rows = per * cap
    run = groups // CHUNKS
    hidden = 2 * half
    n = PARTS * tok
    step = 256
    mark = 2
    last = sections - 1
    prev, own, after = 0, 1, 2
    s = lax.axis_index("section")
    ex = lax.axis_index("expert")
    core = lax.rem(ex, 2)
    chip = lax.div(ex, 2)
    mate = 2 * chip + (1 - core)
    my_group = lax.div(chip, per)

    def other(j):
        g = lax.rem(my_group + lax.div(j, per), groups)
        return g * per + lax.rem(chip + j, per)

    barrier = pltpu.get_barrier_semaphore()

    def greet(j, carry):
        pl.semaphore_signal(
            barrier, inc=1, device_id={"expert": 2 * other(j) + core}, device_id_type=MESH
        )
        return carry

    turns = jnp.where(s == last, micro, 2 * micro)

    lax.fori_loop(1, chips, greet, 0)
    pl.semaphore_signal(barrier, inc=1, device_id={"expert": mate}, device_id_type=MESH)

    @pl.when(s > 0)
    def _():
        pl.semaphore_signal(barrier, inc=1, device_id={"section": s - 1}, device_id_type=MESH)

    @pl.when(s < last)
    def _():
        pl.semaphore_signal(barrier, inc=1, device_id={"section": s + 1}, device_id_type=MESH)

    local = [
        pltpu.make_async_copy(w_gate_ref, wg.at[:, :half], w_local.at[0]),
        pltpu.make_async_copy(w_up_ref, wu.at[:, :half], w_local.at[1]),
        pltpu.make_async_copy(w_down_ref, wd.at[:half, :], w_local.at[2]),
    ]
    for copy in local:
        copy.start()

    def columns(which, ref):
        cols[which] = jnp.transpose(ref[:, : 2 * n])

    def build(which, m):
        for k in range(2):
            at = k * n
            sub = cols[which, at : at + n, :][:, m : m + 1]
            ids = lax.broadcasted_iota(jnp.int32, (n, chips * blk), 1)
            collect[which, m, at : at + n, :] = jnp.where(
                ids == sub.astype(jnp.int32), 1.0, 0.0
            ).astype(BF16)

    def build_spread(m, ref=info_ref, place=0):
        for k in range(2):
            at = k * n
            lane = ref[m : m + 1, at : at + n].astype(jnp.int32)
            ids = lax.broadcasted_iota(jnp.int32, (chips * blk, n), 0)
            spread[place + m, :, at : at + n] = jnp.where(ids == lane, 1.0, 0.0).astype(BF16)

    build_spread(0)
    ahead = lax.convert_element_type(s > 0, jnp.int32)
    behind = lax.convert_element_type(s < last, jnp.int32)
    pl.semaphore_wait(barrier, chips + ahead + behind)

    @pl.when(s > 0)
    def _():
        pl.semaphore_signal(entered.at[1], inc=1, device_id={"section": s - 1}, device_id_type=MESH)

    @pl.when(s < last)
    def _():
        pl.semaphore_signal(entered.at[0], inc=1, device_id={"section": s + 1}, device_id_type=MESH)

    remote = [
        pltpu.make_async_remote_copy(
            src, dst, w_send.at[i], w_recv.at[i], device_id={"expert": mate}, device_id_type=MESH
        )
        for i, (src, dst) in enumerate(
            (
                (w_gate_ref, wg.at[:, half:]),
                (w_up_ref, wu.at[:, half:]),
                (w_down_ref, wd.at[half:, :]),
            )
        )
    ]
    for copy in remote:
        copy.start()

    def tell(slot, to):
        return pltpu.make_async_remote_copy(
            info_ref,
            info_near.at[slot],
            i_send.at[slot],
            i_recv.at[slot],
            device_id={"section": to},
            device_id_type=MESH,
        )

    @pl.when(s < last)
    def _():
        tell(0, s + 1).start()

    @pl.when(s > 0)
    def _():
        tell(1, s - 1).start()

    def hop(src, dst, m, kind, to):
        return pltpu.make_async_remote_copy(
            src.at[m],
            dst.at[m],
            x_send.at[kind, m],
            x_recv.at[kind, m],
            device_id={"section": to},
            device_id_type=MESH,
        )

    h_on = functools.partial(hop, h_in, h_prev, kind=0)
    h_back = functools.partial(hop, h_in, h_next, kind=1)
    g_back = functools.partial(hop, g_in, g_next, kind=2)
    o_on = functools.partial(hop, g_in, o_in, kind=3)

    def send_wait(buf, u, sem, count):
        view = buf.at[u, pl.ds(0, count)]
        pltpu.make_async_copy(view, view, sem.at[u]).wait()

    def group_wait(buf, u, i, sem):
        g = lax.rem(my_group + groups - i, groups)
        view = buf.at[u, pl.ds(g * per, per)]
        pltpu.make_async_copy(view, view, sem.at[u, g]).wait()
        return g

    def fill(u, sel, value):
        send_a[u] = mm(sel, value).reshape(chips, blk, part).astype(BF16)

    def dispatch(u):
        @pl.when(jnp.logical_or(core == 1, u > 0))
        def _():
            pl.semaphore_wait(turn, 1)

        def one(j, carry):
            d = other(j)
            pltpu.make_async_remote_copy(
                send_a.at[u, d],
                recv_a.at[u, chip],
                a_send.at[u],
                a_recv.at[u, my_group],
                device_id={"expert": 2 * d + core},
                device_id_type=MESH,
            ).start()
            return carry

        lax.fori_loop(1, chips, one, 0)
        pltpu.make_async_copy(send_a.at[u, chip], recv_a.at[u, chip], a_recv.at[u, my_group]).start()

    def dispatch_last(m):
        def one(j, carry):
            d = other(j)
            pltpu.make_async_remote_copy(
                send_a.at[2 * micro + m, d],
                recv_a.at[micro + m, chip],
                a_send.at[2 * micro + m],
                a_recv.at[micro + m, my_group],
                device_id={"section": last, "expert": 2 * d + core},
                device_id_type=MESH,
            ).start()
            return carry

        lax.fori_loop(0, chips, one, 0)

    def arrive(u, c):
        def one(t, carry):
            i = c * run + t
            g = group_wait(recv_a, u, i, a_recv)

            got = recv_a[u, pl.ds(g * per, per)].astype(F32).reshape(per * blk, part).astype(BF16)
            sorted_rows = mm(perm_ref[...], got).astype(BF16)
            for q in range(PARTS):
                rows[pl.ds(t * grp_rows, grp_rows), q * part : (q + 1) * part] = sorted_rows[
                    q * grp_rows : (q + 1) * grp_rows
                ]
            return carry

        lax.fori_loop(0, run, one, 0)

    def give_back(u, c, to, slot):
        def one(t, carry):
            g = lax.rem(my_group + groups - c * run - t, groups)
            got = mm(perm_t_ref[...], pieces[t])
            send_b[u, pl.ds(g * per, per)] = got.reshape(per, blk, part).astype(BF16)

            def block(j, inner):
                d = g * per + lax.rem(chip + j, per)

                @pl.when(jnp.logical_or(d != chip, to != s))
                def _():
                    pltpu.make_async_remote_copy(
                        send_b.at[u, d],
                        recv_b.at[slot, chip],
                        b_send.at[u],
                        b_recv.at[slot, my_group],
                        device_id={"section": to, "expert": 2 * d + core},
                        device_id_type=MESH,
                    ).start()

                return inner

            return lax.fori_loop(0, per, block, carry)

        lax.fori_loop(0, run, one, 0)

        @pl.when((u < turns - 1 + (1 - core)) & (c == mark))
        def _():
            pl.semaphore_signal(turn, inc=1, device_id={"expert": mate}, device_id_type=MESH)

        @pl.when((to == s) & (c == 0))
        def _():
            pltpu.make_async_copy(
                send_b.at[u, chip], recv_b.at[slot, chip], b_recv.at[slot, my_group]
            ).start()

    def wait_back(slot):
        def one(i, carry):
            group_wait(recv_b, slot, i, b_recv)
            return carry

        lax.fori_loop(0, groups, one, 0)
        return recv_b[slot].astype(F32).reshape(chips * blk, part).astype(BF16)

    def put_pieces(q, value):
        for t in range(run):
            pieces[t, pl.ds(q * grp_rows, grp_rows), :] = value[t * grp_rows : (t + 1) * grp_rows]

    def gate_column(which, m):
        return jnp.where(m == 0, cols[which][:, micro : micro + 1], cols[which][:, micro + 1 : micro + 2])

    def inverse_rms(h):
        total = jnp.sum(jnp.sum(h * h, axis=-1, keepdims=True), axis=0)
        return lax.rsqrt(total / width + EPS)

    def mix(h, slot, which, m):
        picked = mm(collect[which, m], wait_back(slot)) * gate_column(which, m)
        mixture = picked[:n] + picked[n:]
        return (h.astype(F32) + mixture.reshape(PARTS, tok, part)).astype(BF16)

    def grad(g, h, gain, slot, which, m):
        sel = collect[which, m, :n] + collect[which, m, n:]
        total = mm(sel, wait_back(slot)).reshape(PARTS, tok, part)
        h = h.astype(F32)
        inv = inverse_rms(h)
        weighted = total * jnp.stack([gain[2 * micro + q : 2 * micro + q + 1, :] for q in range(PARTS)])
        dot = jnp.sum(jnp.sum(h * weighted, axis=-1, keepdims=True), axis=0) / width
        change = inv[None] * weighted - h * (inv * inv * inv * dot)[None]
        return (g.astype(F32) + change).astype(BF16)


    def later_tables():
        columns(own, info_ref)
        for m in range(micro):
            build(own, m)

        @pl.when(s < last)
        def _():
            tell(1, s).wait_recv()
            columns(after, info_near.at[1])
            for m in range(micro):
                build(after, m)

            @pl.when(s == last - 1)
            def _():
                for m in range(micro):
                    build_spread(m, info_near.at[1], micro)

    @pl.when(s > 0)
    def _():
        build_spread(1)
        pl.semaphore_wait(entered.at[0], 1)
        tell(0, s).wait_recv()
        columns(prev, info_near.at[0])
        for m in range(micro):
            build(prev, m)
        later_tables()

    def forward(m, carry):
        u = m

        @pl.when(s == 0)
        def _():
            for q in range(PARTS):
                h_in[m, q] = tokens_ref[m, :, q * part : (q + 1) * part]

        @pl.when(s > 0)
        def _():
            h_on(m=m, to=s).wait_recv()
            h_in[m] = mix(h_prev[m], m, prev, m)

        inv = inverse_rms(h_in[m].astype(F32))
        for q in range(PARTS):
            gain = info_ref[2 * micro + q : 2 * micro + q + 1, :]
            stage[pl.ds(q * tok, tok), :] = (h_in[m, q].astype(F32) * inv * gain).astype(BF16)
        fill(u, spread[m, :, :n] + spread[m, :, n:], stage[:n, :])
        dispatch(u)

        @pl.when(s < last)
        def _():
            h_on(m=m, to=s + 1).start()

        @pl.when(s > 0)
        def _():
            h_back(m=m, to=s - 1).start()

        @pl.when(m == 0)
        def _():
            for copy in local:
                copy.wait()
            for copy in remote:
                copy.wait_recv()

            @pl.when(s == 0)
            def _():
                build_spread(1)

            @pl.when(s < last)
            def _():
                pl.semaphore_wait(entered.at[1], 1)

        def chunk(c, carry):
            arrive(u, c)

            def first(i, carry):
                at = pl.ds(pl.multiple_of(i * step, step), step)
                gate = mm(rows[...], wg[:, at])
                up = mm(rows[...], wu[:, at])
                pre_g[m, c, i] = gate
                pre_u[m, c, i] = up
                act_a[:, at] = (gate * jax.nn.sigmoid(gate) * up).astype(BF16)
                return carry

            lax.fori_loop(0, hidden // step, first, 0)

            def second(q, carry):
                at = pl.ds(pl.multiple_of(q * part, part), part)
                put_pieces(q, mm(act_a[...], wd[:, at]).astype(BF16))
                return carry

            lax.fori_loop(0, PARTS, second, 0)
            give_back(u, c, jnp.where(s == last, last - 1, s + 1), m + micro * (1 - behind))
            return carry

        lax.fori_loop(0, CHUNKS, chunk, 0)

        return carry

    lax.fori_loop(0, micro, forward, 0)

    def scale(value, which, m):
        upstream = value.astype(F32).reshape(n, part)
        gates = gate_column(which, m)
        stage[:n, :] = (gates[:n] * upstream).astype(BF16)
        stage[n:, :] = (gates[n:] * upstream).astype(BF16)

    @pl.when(s == last - 1)
    def _():
        def one(m, carry):
            h_back(m=m, to=s).wait_recv()
            g_next[m] = mix(h_next[m], micro + m, after, m)
            scale(g_next[m], after, m)
            fill(2 * micro + m, spread[micro + m], stage[...])
            dispatch_last(m)
            return carry

        lax.fori_loop(0, micro, one, 0)

    @pl.when(s == 0)
    def _():
        later_tables()

    def backward(m, carry):
        u = micro + m

        @pl.when(s < last - 1)
        def _():
            g_back(m=m, to=s).wait_recv()
            h_back(m=m, to=s).wait_recv()

        @pl.when(s < last)
        def _():
            g_in[m] = grad(g_next[m], h_next[m], info_near.at[1], 2 * micro + m, after, m)
            scale(g_in[m], own, m)
            fill(u, spread[m], stage[...])
            dispatch(u)

        @pl.when((s > 0) & (s < last))
        def _():
            g_back(m=m, to=s - 1).start()

        @pl.when(s < last)
        def _():
            o_on(m=m, to=s + 1).start()

        def chunk(c, carry):
            arrive(u, c)

            def first(i, carry):
                at = pl.ds(pl.multiple_of(i * step, step), step)
                grad_hidden = mm_nt(rows[...], wd[at, :])
                gate = pre_g[m, c, i]
                up = pre_u[m, c, i]
                logistic = jax.nn.sigmoid(gate)
                slope = logistic * (1.0 + gate * (1.0 - logistic))
                act_a[:, at] = (grad_hidden * up * slope).astype(BF16)
                act_b[:, at] = (grad_hidden * gate * logistic).astype(BF16)
                return carry

            lax.fori_loop(0, hidden // step, first, 0)

            def second(q, carry):
                at = pl.ds(pl.multiple_of(q * part, part), part)
                value = mm_nt(act_a[...], wg[at, :]) + mm_nt(act_b[...], wu[at, :])
                put_pieces(q, value.astype(BF16))
                return carry

            lax.fori_loop(0, PARTS, second, 0)
            give_back(u, c, jnp.maximum(s - 1, 0), 2 * micro + m + micro * (1 - ahead))
            return carry

        lax.fori_loop(0, CHUNKS, chunk, 0)

        @pl.when(s == 0)
        def _():
            value = grad(g_in[m], h_in[m], info_ref, 3 * micro + m, own, m)
            for q in range(PARTS):
                out_ref[m, :, q * part : (q + 1) * part] = value[q]

        return carry

    lax.fori_loop(0, micro, backward, 0)

    @pl.when(s > 0)
    def _():
        for m in range(micro):
            o_on(m=m, to=s).wait_recv()
            for q in range(PARTS):
                out_ref[m, :, q * part : (q + 1) * part] = o_in[m, q]

    for copy in remote:
        copy.wait_send()

    @pl.when(s < last)
    def _():
        tell(0, s).wait_send()

    @pl.when(s > 0)
    def _():
        tell(1, s).wait_send()

    def drain(u, carry):
        @pl.when(u < turns)
        def _():
            send_wait(send_a, u, a_send, chips - 1)

        stays = (u >= micro) & (s == 0)

        @pl.when(stays)
        def _():
            send_wait(send_b, u, b_send, chips - 1)

        @pl.when(jnp.logical_not(stays))
        def _():
            send_wait(send_b, u, b_send, chips)

        return carry

    lax.fori_loop(0, 2 * micro, drain, 0)
    for m in range(micro):

        @pl.when(s < last)
        def _():
            h_on(m=m, to=s).wait_send()
            o_on(m=m, to=s).wait_send()

        @pl.when(s > 0)
        def _():
            h_back(m=m, to=s).wait_send()

        @pl.when((s > 0) & (s < last))
        def _():
            g_back(m=m, to=s).wait_send()

        @pl.when(s == last - 1)
        def _():
            send_wait(send_a, 2 * micro + m, a_send, chips)


def body(tokens, norm_gain, w_gate, w_up, w_down, route_ids, route_gates):
    sections = lax.axis_size("section")
    chips = lax.axis_size("expert") // 2
    micro, tok, width = tokens.shape
    top = route_ids.shape[-1]
    half = w_gate.shape[-1]
    hidden = 2 * half
    cap = max(2, (4 * tok * top + 3 * chips - 1) // (3 * chips))
    blk = PARTS * cap
    part = width // PARTS
    groups = 4
    per = chips // groups
    grp = per * cap
    units = 2 * micro
    chunk_rows = chips * cap // CHUNKS

    flat = route_ids[0].reshape(micro, tok * top)
    onehot = (flat[:, :, None] == jnp.arange(chips, dtype=jnp.int32)).astype(jnp.int32)
    before = jnp.cumsum(onehot, axis=1) - onehot
    position = jnp.sum(before * onehot, axis=-1)
    first = (flat * blk + position).reshape(micro, tok, top).transpose(0, 2, 1)
    offset = jnp.arange(PARTS, dtype=jnp.int32) * cap
    target = (first[:, :, None, :] + offset[None, None, :, None]).reshape(micro, top * PARTS * tok)
    gates = route_gates[0].transpose(0, 2, 1)
    gates = jnp.broadcast_to(gates[:, :, None, :], (micro, top, PARTS, tok)).reshape(micro, -1)
    pad = ((0, 0), (0, part - top * PARTS * tok))
    info = jnp.concatenate(
        [
            jnp.pad(target.astype(F32), pad),
            jnp.pad(gates, pad),
            norm_gain.reshape(PARTS, part),
            jnp.zeros((16 - 2 * micro - PARTS, part), F32),
        ]
    )

    src = np.arange(per * blk)
    dest = (src % blk // cap) * grp + src // blk * cap + src % cap
    perm_t = jnp.asarray(dest[:, None] == src[None, :], dtype=BF16)
    perm = jnp.asarray(src[:, None] == dest[None, :], dtype=BF16)

    dims = (sections, chips, cap, tok, width, micro, groups, half)
    vmem = pl.BlockSpec(memory_space=pltpu.VMEM)
    hbm = pl.BlockSpec(memory_space=pl.ANY)
    dma = pltpu.SemaphoreType.DMA
    result = pl.pallas_call(
        functools.partial(kernel, dims),
        out_shape=jax.ShapeDtypeStruct((micro, tok, width), BF16),
        in_specs=[vmem] * 4 + [hbm] * 3,
        out_specs=vmem,
        scratch_shapes=[
            pltpu.VMEM((width, hidden), BF16),
            pltpu.VMEM((width, hidden), BF16),
            pltpu.VMEM((hidden, width), BF16),
            pltpu.VMEM((2, 16, part), F32),
            pltpu.VMEM((3, top * PARTS * tok, 16), F32),
        ]
        + [pltpu.VMEM((micro, PARTS, tok, part), BF16)] * 6
        + [
            pltpu.VMEM((units + micro, chips, blk, part), BF16),
            pltpu.VMEM((units, chips, blk, part), BF16),
            pltpu.VMEM((units, chips, blk, part), BF16),
            pltpu.VMEM((2 * units, chips, blk, part), BF16),
            pltpu.VMEM((2 * micro, chips * blk, top * PARTS * tok), BF16),
            pltpu.VMEM((3, micro, top * PARTS * tok, chips * blk), BF16),
            pltpu.VMEM((top * PARTS * tok, part), BF16),
            pltpu.VMEM((groups // CHUNKS, PARTS * grp, part), BF16),
            pltpu.VMEM((chunk_rows, width), BF16),
            pltpu.VMEM((micro, CHUNKS, hidden // 256, chunk_rows, 256), F32),
            pltpu.VMEM((micro, CHUNKS, hidden // 256, chunk_rows, 256), F32),
            pltpu.VMEM((chunk_rows, hidden), BF16),
            pltpu.VMEM((chunk_rows, hidden), BF16),
            dma((3,)),
            dma((3,)),
            dma((3,)),
            dma((2,)),
            dma((2,)),
            dma((units + micro,)),
            dma((units, groups)),
            dma((units,)),
            dma((2 * units, groups)),
            dma((4, micro)),
            dma((4, micro)),
            pltpu.SemaphoreType.REGULAR,
            pltpu.SemaphoreType.REGULAR((2,)),
        ],
        compiler_params=pltpu.CompilerParams(
            collective_id=0, has_side_effects=True, vmem_limit_bytes=60 * 1024 * 1024
        ),
        name="relay",
    )(
        tokens,
        info,
        perm,
        perm_t,
        w_gate[0],
        w_up[0],
        w_down[0],
    )
    return result[None]


def solution(mesh):
    in_specs = (
        P(None, "expert", None),
        P("section", None),
        P("section", None, "expert"),
        P("section", None, "expert"),
        P("section", "expert", None),
        P("section", None, "expert", None),
        P("section", None, "expert", None),
    )
    out_specs = P("section", None, "expert", None)
    return jax.shard_map(body, mesh=mesh, in_specs=in_specs, out_specs=out_specs, check_vma=False)
```
